128 devices in a mesh: gx: 32 (over z_lo, y, x), gy: 4 (over z_hi, core).
Axes of the slice: x: 4, y: 4, z: 4 (z_hi: 2, z_lo: 2; z = z_hi * 2 + z_lo), core: 2. Of those that a mesh axis runs over, the one named last changes fastest.
Arguments:
- tokens: bfloat16 [512, 256, 1024], P(('gx', 'gy')), may hold values from -128 to 128, as said below
- slot_params: bfloat16 [1024, 128], replicated, may hold values from -1 to 1, as said below
- expand_weight: bfloat16 [128, 1024, 2048], P(('gx', 'gy')), may hold values from -0.1875 to 0.1875
- shrink_weight: bfloat16 [128, 2048, 1024], P(('gx', 'gy')), may hold values from -0.125 to 0.125
- cotangent: bfloat16 [512, 256, 1024], P(('gx', 'gy')), may hold values from -6 to 6
Outputs:
- layer_out: bfloat16 [512, 256, 1024], P(('gx', 'gy'))
- grad_tokens: bfloat16 [512, 256, 1024], P(('gx', 'gy'))
- grad_phi: float32 [1024, 128], replicated
- grad_expand: bfloat16 [128, 1024, 2048], P(('gx', 'gy'))
- grad_shrink: bfloat16 [128, 2048, 1024], P(('gx', 'gy'))
The draws below stay inside these ranges and needn't reach their ends.
Inputs may be any that keep to these rules, and one draw needn't show every extreme that they name: `tokens`: finite values. `slot_params`: finite values.
All inputs are finite; a program needn't handle non-finite values.
Results may differ from the reference program's by a relative error of at most 0.02.
Values may be sent and summed in bfloat16 or wider, within the bound.
No kernel may reach another device: no remote copies, remote signals or barrier semaphores. Data moves between devices by JAX's collectives and lax.ppermute only.
A program may use at most 128 MiB of HBM per device.

```python
import math
import jax
import jax.numpy as jnp
from jax import lax

D = 1024
FF = 2048
PATCH = 256
EXPERTS = 128
IMAGES = 512


def slot_pattern(key):
    base_key = jax.random.fold_in(key, 11)
    sign_key, scale_key = jax.random.split(base_key)
    half_signs = jnp.where(jax.random.bernoulli(sign_key, 0.5, (D, EXPERTS // 2)), 1.0, -1.0).astype(jnp.float32)
    upper = (jnp.arange(D) < D // 2)[:, None]
    partner = jnp.where(upper, half_signs, -half_signs)
    signs = jnp.stack([half_signs, partner], axis=2).reshape(D, EXPERTS)
    scales = jnp.exp(jax.random.uniform(scale_key, (EXPERTS,), jnp.float32, math.log(0.5), math.log(2.5)))
    return (signs, scales)


def draw_slot_params(key, part):
    signs, scales = slot_pattern(key)
    return (signs * scales[None, :] / math.sqrt(D)).astype(jnp.bfloat16)


def draw_tokens(key, part):
    base_key = jax.random.fold_in(key, 23)
    scale_key, value_key = jax.random.split(base_key, 2)
    row_scale = jnp.exp(jax.random.uniform(scale_key, (IMAGES, PATCH, 1), jnp.float32, math.log(0.5), math.log(5.0)))
    values = jax.random.normal(value_key, (IMAGES, PATCH, D), jnp.float32) * row_scale
    return jnp.clip(values, -128.0, 128.0).astype(jnp.bfloat16)


def block_scale(rng, dims, shards, smallest, largest):
    def one(axis_at, parts):
        steps = jax.random.uniform(jax.random.fold_in(jax.random.fold_in(rng, 6), axis_at), (parts,), jnp.float32, smallest / len(shards), largest / len(shards))
        return jnp.repeat(jnp.exp(steps), dims[axis_at] // parts).reshape((-1,) + (1,) * (len(dims) - axis_at - 1))

    gain = one(*shards[0])
    for cut in shards[1:]:
        gain = gain * one(*cut)
    return gain


def bell_draw(key, extent, width, most, cuts=(), kind=jnp.bfloat16):
    entries = jax.random.normal(key, extent, jnp.float32) * width
    if len(cuts) > 0:
        entries = block_scale(key, extent, cuts, -0.22, 0.18) * entries
    return jnp.clip(entries, min=-most, max=most).astype(kind)


def setup_inputs(seed: int = 0) -> dict:
    arg_keys = jax.random.split(jax.random.key(seed), 6)
    tokens = draw_tokens(jax.random.fold_in(arg_keys[5], 71), 0)
    slot_params = draw_slot_params(jax.random.fold_in(arg_keys[5], 71), 0)
    expand_weight = bell_draw(arg_keys[2], (EXPERTS, D, FF), D ** -0.5, 0.1875, ((0, 128),))
    shrink_weight = bell_draw(arg_keys[3], (EXPERTS, FF, D), FF ** -0.5, 0.125, ((0, 128),))
    cotangent = bell_draw(arg_keys[4], (IMAGES, PATCH, D), 1.0, 6.0, ((0, 128),))
    return dict(tokens=tokens, slot_params=slot_params, expand_weight=expand_weight, shrink_weight=shrink_weight, cotangent=cotangent)


def gelu_value(values_in):
    return 0.5 * values_in * (1.0 + jax.scipy.special.erf(values_in * 0.7071067811865476))


def gelu_slope(values_in):
    cumulative = 0.5 * (1.0 + jax.scipy.special.erf(values_in * 0.7071067811865476))
    return cumulative + values_in * jnp.exp(-0.5 * values_in * values_in) * 0.3989422804014327


def route_weights(one_image, slot_params):
    logits = jnp.dot(one_image, slot_params, preferred_element_type=jnp.float32)
    return jax.nn.softmax(logits, axis=0), jax.nn.softmax(logits, axis=1)


def reference(tokens, slot_params, expand_weight, shrink_weight, cotangent):
    def forward_slots(one_image):
        dispatch_prob, unused_prob = route_weights(one_image, slot_params)
        return jnp.dot(dispatch_prob.astype(jnp.bfloat16).T, one_image,
                       preferred_element_type=jnp.float32).astype(jnp.bfloat16)

    slot_in = lax.map(forward_slots, tokens)
    by_expert = jnp.transpose(slot_in, (1, 0, 2))

    def expert_forward(inputs_tuple):
        slot_rows, expand, shrink = inputs_tuple
        hidden = jnp.dot(slot_rows, expand, preferred_element_type=jnp.float32)
        activated = gelu_value(hidden).astype(jnp.bfloat16)
        return jnp.dot(activated, shrink, preferred_element_type=jnp.float32).astype(jnp.bfloat16)

    expert_out = lax.map(expert_forward, (by_expert, expand_weight, shrink_weight))
    slot_out = jnp.transpose(expert_out, (1, 0, 2))

    def combine_step(inputs_tuple):
        one_image, outputs_image, grad_image = inputs_tuple
        unused_prob, combine_prob = route_weights(one_image, slot_params)
        combine = combine_prob.astype(jnp.bfloat16)
        layer_out = jnp.dot(combine, outputs_image, preferred_element_type=jnp.float32).astype(jnp.bfloat16)
        grad_combine = jnp.dot(grad_image, outputs_image.T, preferred_element_type=jnp.float32)
        grad_slot_out = jnp.dot(combine.T, grad_image, preferred_element_type=jnp.float32).astype(jnp.bfloat16)
        return layer_out, grad_combine, grad_slot_out

    layer_out, grad_combine, grad_slot_out = lax.map(combine_step, (tokens, slot_out, cotangent))
    grad_by_expert = jnp.transpose(grad_slot_out, (1, 0, 2))

    def expert_backward(inputs_tuple):
        slot_rows, grad_rows, expand, shrink = inputs_tuple
        hidden = jnp.dot(slot_rows, expand, preferred_element_type=jnp.float32)
        activated = gelu_value(hidden).astype(jnp.bfloat16)
        grad_activated = jnp.dot(grad_rows, shrink.T, preferred_element_type=jnp.float32)
        grad_shrink = jnp.dot(activated.T, grad_rows, preferred_element_type=jnp.float32).astype(jnp.bfloat16)
        grad_hidden = (grad_activated * gelu_slope(hidden)).astype(jnp.bfloat16)
        grad_expand = jnp.dot(slot_rows.T, grad_hidden, preferred_element_type=jnp.float32).astype(jnp.bfloat16)
        grad_input = jnp.dot(grad_hidden, expand.T, preferred_element_type=jnp.float32).astype(jnp.bfloat16)
        return grad_input, grad_expand, grad_shrink

    grad_input, grad_expand, grad_shrink = lax.map(
        expert_backward, (by_expert, grad_by_expert, expand_weight, shrink_weight))
    grad_slot_in = jnp.transpose(grad_input, (1, 0, 2))

    def router_backward(inputs_tuple):
        one_image, grad_in_image, grad_comb_image = inputs_tuple
        dispatch_prob, combine_prob = route_weights(one_image, slot_params)
        grad_dispatch = jnp.dot(one_image, grad_in_image.T, preferred_element_type=jnp.float32)
        part_dispatch = dispatch_prob * (grad_dispatch - jnp.sum(dispatch_prob * grad_dispatch, axis=0, keepdims=True))
        part_combine = combine_prob * (grad_comb_image - jnp.sum(combine_prob * grad_comb_image, axis=1, keepdims=True))
        grad_logits = (part_dispatch + part_combine).astype(jnp.bfloat16)
        grad_image = (jnp.dot(dispatch_prob.astype(jnp.bfloat16), grad_in_image, preferred_element_type=jnp.float32)
                      + jnp.dot(grad_logits, slot_params.T, preferred_element_type=jnp.float32)).astype(jnp.bfloat16)
        phi_term = jnp.dot(one_image.T, grad_logits, preferred_element_type=jnp.float32)
        return grad_image, phi_term

    grad_tokens, phi_terms = lax.map(router_backward, (tokens, grad_slot_in, grad_combine))
    grad_phi = jnp.sum(phi_terms, axis=0)
    return layer_out, grad_tokens, grad_phi, grad_expand, grad_shrink
```

```python
import jax
import jax.numpy as jnp
from jax import lax
from jax.sharding import PartitionSpec as P

AXES = ("gx", "gy")


def gelu_value(values_in):
    return 0.5 * values_in * (1.0 + jax.scipy.special.erf(values_in * 0.7071067811865476))


def gelu_slope(values_in):
    cumulative = 0.5 * (1.0 + jax.scipy.special.erf(values_in * 0.7071067811865476))
    return cumulative + values_in * jnp.exp(-0.5 * values_in * values_in) * 0.3989422804014327


def exchange(chunks):
    return lax.all_to_all(chunks, AXES, split_axis=0, concat_axis=0, tiled=True)


def sum_everywhere(partial):
    parts = lax.axis_size(AXES)
    rows, columns = partial.shape
    pieces = partial.astype(jnp.bfloat16).reshape(parts, rows // parts, columns)
    own = jnp.sum(exchange(pieces).astype(jnp.float32), axis=0).astype(jnp.bfloat16)
    copies = jnp.broadcast_to(own[None], (parts,) + own.shape)
    return exchange(copies).astype(jnp.float32).reshape(rows, columns)


def body(tokens, slot_params, expand_weight, shrink_weight, cotangent):
    images = tokens.shape[0]
    model_width = tokens.shape[2]
    logits = jnp.einsum("ipd,ds->ips", tokens, slot_params, preferred_element_type=jnp.float32)
    dispatch_prob = jax.nn.softmax(logits, axis=1)
    combine_prob = jax.nn.softmax(logits, axis=2)
    dispatch = dispatch_prob.astype(jnp.bfloat16)
    combine = combine_prob.astype(jnp.bfloat16)
    slot_in = jnp.einsum(
        "ips,ipd->sid", dispatch, tokens, preferred_element_type=jnp.float32
    ).astype(jnp.bfloat16)
    grad_slot_out = jnp.einsum(
        "ips,ipd->sid", combine, cotangent, preferred_element_type=jnp.float32
    ).astype(jnp.bfloat16)
    arrived = exchange(jnp.concatenate([slot_in, grad_slot_out], axis=1))
    expert_rows = arrived[:, :images].reshape(-1, model_width)
    grad_rows = arrived[:, images:].reshape(-1, model_width)
    expand = expand_weight[0]
    shrink = shrink_weight[0]
    hidden = jnp.dot(expert_rows, expand, preferred_element_type=jnp.float32)
    activated = gelu_value(hidden).astype(jnp.bfloat16)
    result_rows = jnp.dot(activated, shrink, preferred_element_type=jnp.float32).astype(
        jnp.bfloat16
    )
    grad_activated = jnp.dot(grad_rows, shrink.T, preferred_element_type=jnp.float32)
    grad_hidden = (grad_activated * gelu_slope(hidden)).astype(jnp.bfloat16)
    grad_input_rows = jnp.dot(grad_hidden, expand.T, preferred_element_type=jnp.float32).astype(
        jnp.bfloat16
    )
    returned = exchange(
        jnp.concatenate(
            [
                result_rows.reshape(-1, images, model_width),
                grad_input_rows.reshape(-1, images, model_width),
            ],
            axis=1,
        )
    )
    slot_out = returned[:, :images]
    grad_slot_in = returned[:, images:]
    grad_shrink = jnp.dot(activated.T, grad_rows, preferred_element_type=jnp.float32).astype(
        jnp.bfloat16
    )
    grad_expand = jnp.dot(expert_rows.T, grad_hidden, preferred_element_type=jnp.float32).astype(
        jnp.bfloat16
    )
    grad_combine = jnp.einsum(
        "ipd,sid->ips", cotangent, slot_out, preferred_element_type=jnp.float32
    )
    grad_dispatch = jnp.einsum(
        "ipd,sid->ips", tokens, grad_slot_in, preferred_element_type=jnp.float32
    )
    part_dispatch = dispatch_prob * (
        grad_dispatch - jnp.sum(dispatch_prob * grad_dispatch, axis=1, keepdims=True)
    )
    part_combine = combine_prob * (
        grad_combine - jnp.sum(combine_prob * grad_combine, axis=2, keepdims=True)
    )
    grad_logits = (part_dispatch + part_combine).astype(jnp.bfloat16)
    phi_term = jnp.einsum("ipd,ips->ds", tokens, grad_logits, preferred_element_type=jnp.float32)
    grad_phi = sum_everywhere(phi_term)
    layer_out = jnp.einsum(
        "ips,sid->ipd", combine, slot_out, preferred_element_type=jnp.float32
    ).astype(jnp.bfloat16)
    grad_tokens = (
        jnp.einsum("ips,sid->ipd", dispatch, grad_slot_in, preferred_element_type=jnp.float32)
        + jnp.einsum("ips,ds->ipd", grad_logits, slot_params, preferred_element_type=jnp.float32)
    ).astype(jnp.bfloat16)
    return (layer_out, grad_tokens, grad_phi, grad_expand[None], grad_shrink[None])


def solution(mesh):
    placed = (
        P(("gx", "gy"), None, None),
        P(),
        P(("gx", "gy"), None, None),
        P(("gx", "gy"), None, None),
        P(("gx", "gy"), None, None),
    )
    return jax.shard_map(
        body,
        mesh=mesh,
        in_specs=placed,
        out_specs=(
            P(("gx", "gy"), None, None),
            P(("gx", "gy"), None, None),
            P(),
            P(("gx", "gy"), None, None),
            P(("gx", "gy"), None, None),
        ),
        check_vma=False,
    )
```

```python
import jax
import jax.numpy as jnp
from jax import lax
from jax.experimental import pallas as pl
from jax.experimental.pallas import tpu as pltpu
from jax.sharding import PartitionSpec as P

AXES = ("gx", "gy")
BF16 = jnp.bfloat16
F32 = jnp.float32
TILE = 256
NN = (((1,), (0,)), ((), ()))
NT = (((1,), (1,)), ((), ()))


def mul(left, right, how=NN):
    return lax.dot_general(left, right, how, preferred_element_type=F32)


def exchange(chunks):
    return lax.all_to_all(chunks, AXES, split_axis=0, concat_axis=0, tiled=True)


def one_hot_rows(kinds, grouped_to_mixed):
    span = TILE // kinds
    row = lax.broadcasted_iota(jnp.int32, (TILE, TILE), 0)
    column = lax.broadcasted_iota(jnp.int32, (TILE, TILE), 1)
    if grouped_to_mixed:
        source = (row % kinds) * span + row // kinds
    else:
        source = (row % span) * kinds + row // span
    return jnp.where(column == source, 1.0, 0.0).astype(BF16)


def pre_kernel(tokens_ref, cotangent_ref, params_ref, send_ref, dispatch_ref, combine_ref, rows_ref):
    step = pl.program_id(0)
    images = rows_ref.shape[0] // 2

    @pl.when(step < images)
    def _():
        one_image = tokens_ref[0]
        logits = mul(one_image, params_ref[...])
        down = jnp.exp(logits - jnp.max(logits, axis=0, keepdims=True))
        down = down / jnp.sum(down, axis=0, keepdims=True)
        across = jnp.exp(logits - jnp.max(logits, axis=1, keepdims=True))
        across = across / jnp.sum(across, axis=1, keepdims=True)
        dispatch_ref[0] = down
        combine_ref[0] = across
        rows_ref[step] = mul(down.T.astype(BF16), one_image).astype(BF16)
        rows_ref[images + step] = mul(across.T.astype(BF16), cotangent_ref[0]).astype(BF16)

    @pl.when(step >= images)
    def _():
        kinds = 2 * images
        span = TILE // kinds
        block = step - images
        grouped = rows_ref[:, pl.ds(block * span, span), :].reshape(TILE, rows_ref.shape[2])
        send_ref[...] = mul(one_hot_rows(kinds, True), grouped).astype(BF16)


def pre(tokens, cotangent, params):
    images, patches, width = tokens.shape
    slots = params.shape[1]
    kinds = 2 * images
    blocks = slots * kinds // TILE

    def image_map(step):
        return (jnp.minimum(step, images - 1), 0, 0)

    return pl.pallas_call(
        pre_kernel,
        grid=(images + blocks,),
        in_specs=[
            pl.BlockSpec((1, patches, width), image_map),
            pl.BlockSpec((1, patches, width), image_map),
            pl.BlockSpec((width, slots), lambda step: (0, 0)),
        ],
        out_specs=[
            pl.BlockSpec((TILE, width), lambda step: (jnp.maximum(step - images, 0), 0)),
            pl.BlockSpec((1, patches, slots), image_map),
            pl.BlockSpec((1, patches, slots), image_map),
        ],
        out_shape=[
            jax.ShapeDtypeStruct((slots * kinds, width), BF16),
            jax.ShapeDtypeStruct((images, patches, slots), F32),
            jax.ShapeDtypeStruct((images, patches, slots), F32),
        ],
        scratch_shapes=[pltpu.VMEM((kinds, slots, width), BF16)],
        compiler_params=pltpu.CompilerParams(vmem_limit_bytes=24 << 20),
        name="pre",
    )(tokens, cotangent, params)


def expert_kernel(
    kinds,
    arrived_ref,
    expand_ref,
    shrink_ref,
    send_ref,
    rows_ref,
    grads_ref,
    activated_ref,
    hidden_grad_ref,
    result_ref,
    input_grad_ref,
):
    step = pl.program_id(0)
    last = pl.num_programs(0) - 1
    half = TILE // 2
    blocks = arrived_ref.shape[0] // TILE

    @pl.when(step == 0)
    def _():
        order = one_hot_rows(kinds, False)
        for block in range(blocks):
            grouped = mul(order, arrived_ref[block * TILE : (block + 1) * TILE]).astype(BF16)
            rows_ref[block * half : (block + 1) * half] = grouped[:half]
            grads_ref[block * half : (block + 1) * half] = grouped[half:]

    expand = expand_ref[...]
    shrink = shrink_ref[...]
    hidden = mul(rows_ref[...], expand)
    grad_activated = mul(grads_ref[...], shrink, NT)
    cumulative = 0.5 * (1.0 + lax.erf(hidden * 0.7071067811865476))
    bell = jnp.exp(-0.5 * hidden * hidden) * 0.3989422804014327
    activated = (hidden * cumulative).astype(BF16)
    hidden_grad = (grad_activated * (cumulative + hidden * bell)).astype(BF16)
    activated_ref[...] = activated
    hidden_grad_ref[...] = hidden_grad
    result = mul(activated, shrink)
    input_grad = mul(hidden_grad, expand, NT)

    @pl.when(step == 0)
    def _():
        result_ref[...] = result
        input_grad_ref[...] = input_grad

    @pl.when(step > 0)
    def _():
        result_ref[...] += result
        input_grad_ref[...] += input_grad

    @pl.when(step == last)
    def _():
        order = one_hot_rows(kinds, True)
        for block in range(blocks):
            span = slice(block * half, (block + 1) * half)
            grouped = jnp.concatenate(
                [result_ref[span].astype(BF16), input_grad_ref[span].astype(BF16)], axis=0
            )
            send_ref[block * TILE : (block + 1) * TILE] = mul(order, grouped).astype(BF16)


def expert(arrived, expand, shrink, kinds):
    total, width = arrived.shape
    hidden_width = expand.shape[1]
    rows = total // 2
    chunk = 512
    whole = lambda step: (0, 0)
    return pl.pallas_call(
        lambda *refs: expert_kernel(kinds, *refs),
        grid=(hidden_width // chunk,),
        in_specs=[
            pl.BlockSpec((total, width), whole),
            pl.BlockSpec((width, chunk), lambda step: (0, step)),
            pl.BlockSpec((chunk, width), lambda step: (step, 0)),
        ],
        out_specs=[
            pl.BlockSpec((total, width), whole),
            pl.BlockSpec((rows, width), whole),
            pl.BlockSpec((rows, width), whole),
            pl.BlockSpec((rows, chunk), lambda step: (0, step)),
            pl.BlockSpec((rows, chunk), lambda step: (0, step)),
        ],
        out_shape=[
            jax.ShapeDtypeStruct((total, width), BF16),
            jax.ShapeDtypeStruct((rows, width), BF16),
            jax.ShapeDtypeStruct((rows, width), BF16),
            jax.ShapeDtypeStruct((rows, hidden_width), BF16),
            jax.ShapeDtypeStruct((rows, hidden_width), BF16),
        ],
        scratch_shapes=[pltpu.VMEM((rows, width), F32), pltpu.VMEM((rows, width), F32)],
        compiler_params=pltpu.CompilerParams(vmem_limit_bytes=48 << 20),
        name="expert",
    )(arrived, expand, shrink)


def post_kernel(
    arrived_ref,
    tokens_ref,
    cotangent_ref,
    dispatch_ref,
    combine_ref,
    rows_ref,
    grad_logits_ref,
    phi_ref,
    total_ref,
):
    step = pl.program_id(0)
    kinds, slots, width = rows_ref.shape
    images = kinds // 2

    @pl.when(step == 0)
    def _():
        order = one_hot_rows(kinds, False)
        span = TILE // kinds
        for block in range(slots // span):
            grouped = mul(order, arrived_ref[block * TILE : (block + 1) * TILE]).astype(BF16)
            rows_ref[:, block * span : (block + 1) * span, :] = grouped.reshape(kinds, span, width)

    one_image = tokens_ref[0]
    down = dispatch_ref[0]
    across = combine_ref[0]
    grad_combine = mul(cotangent_ref[0], rows_ref[step], NT)
    grad_dispatch = mul(one_image, rows_ref[images + step], NT)
    part_dispatch = down * (grad_dispatch - jnp.sum(down * grad_dispatch, axis=0, keepdims=True))
    part_combine = across * (grad_combine - jnp.sum(across * grad_combine, axis=1, keepdims=True))
    grad_logits = part_dispatch + part_combine
    grad_logits_ref[0] = grad_logits.astype(BF16)
    term = mul(grad_logits.T.astype(BF16), one_image)

    @pl.when(step == 0)
    def _():
        total_ref[...] = term

    @pl.when(step > 0)
    def _():
        total_ref[...] += term

    @pl.when(step == images - 1)
    def _():
        phi_ref[...] = total_ref[...].T.astype(BF16)


def post(arrived, tokens, cotangent, dispatch, combine):
    images, patches, width = tokens.shape
    slots = dispatch.shape[2]
    kinds = 2 * images
    image_map = lambda step: (step, 0, 0)
    return pl.pallas_call(
        post_kernel,
        grid=(images,),
        in_specs=[
            pl.BlockSpec((slots * kinds, width), lambda step: (0, 0)),
            pl.BlockSpec((1, patches, width), image_map),
            pl.BlockSpec((1, patches, width), image_map),
            pl.BlockSpec((1, patches, slots), image_map),
            pl.BlockSpec((1, patches, slots), image_map),
        ],
        out_specs=[
            pl.BlockSpec((kinds, slots, width), lambda step: (0, 0, 0)),
            pl.BlockSpec((1, patches, slots), image_map),
            pl.BlockSpec((width, slots), lambda step: (0, 0)),
        ],
        out_shape=[
            jax.ShapeDtypeStruct((kinds, slots, width), BF16),
            jax.ShapeDtypeStruct((images, patches, slots), BF16),
            jax.ShapeDtypeStruct((width, slots), BF16),
        ],
        scratch_shapes=[pltpu.VMEM((slots, width), F32)],
        compiler_params=pltpu.CompilerParams(vmem_limit_bytes=24 << 20),
        name="post",
    )(arrived, tokens, cotangent, dispatch, combine)


def tail_kernel(
    out_rows_ref, in_rows_ref, dispatch_ref, combine_ref, grad_logits_ref, params_ref, layer_ref, grad_ref
):
    layer_ref[0] = mul(combine_ref[0].astype(BF16), out_rows_ref[0]).astype(BF16)
    grad_ref[0] = (
        mul(dispatch_ref[0].astype(BF16), in_rows_ref[0])
        + mul(grad_logits_ref[0], params_ref[...], NT)
    ).astype(BF16)


def tail(rows, dispatch, combine, grad_logits, params):
    images, patches, slots = dispatch.shape
    width = rows.shape[2]
    image_map = lambda step: (step, 0, 0)
    out = jax.ShapeDtypeStruct((images, patches, width), BF16)
    return pl.pallas_call(
        tail_kernel,
        grid=(images,),
        in_specs=[
            pl.BlockSpec((1, slots, width), image_map),
            pl.BlockSpec((1, slots, width), lambda step: (images + step, 0, 0)),
            pl.BlockSpec((1, patches, slots), image_map),
            pl.BlockSpec((1, patches, slots), image_map),
            pl.BlockSpec((1, patches, slots), image_map),
            pl.BlockSpec((width, slots), lambda step: (0, 0)),
        ],
        out_specs=[
            pl.BlockSpec((1, patches, width), image_map),
            pl.BlockSpec((1, patches, width), image_map),
        ],
        out_shape=[out, out],
        compiler_params=pltpu.CompilerParams(vmem_limit_bytes=24 << 20),
        cost_estimate=pl.CostEstimate(
            flops=6 * images * patches * slots * width, bytes_accessed=8 << 20, transcendentals=0
        ),
        name="tail",
    )(rows, rows, dispatch, combine, grad_logits, params)


def sum_everywhere(partial):
    parts = lax.axis_size(AXES)
    rows, columns = partial.shape
    pieces = partial.reshape(parts, rows // parts, columns)
    own = jnp.sum(exchange(pieces).astype(F32), axis=0).astype(BF16)
    copies = jnp.broadcast_to(own[None], (parts,) + own.shape)
    return exchange(copies).astype(F32).reshape(rows, columns)


def body(tokens, slot_params, expand_weight, shrink_weight, cotangent):
    images, _, width = tokens.shape
    slots = slot_params.shape[1]
    kinds = 2 * images
    send, dispatch, combine = pre(tokens, cotangent, slot_params)
    arrived = exchange(send.reshape(slots, kinds, width)).reshape(slots * kinds, width)
    send_back, expert_rows, grad_rows, activated, grad_hidden = expert(
        arrived, expand_weight[0], shrink_weight[0], kinds
    )
    returned = exchange(send_back.reshape(slots, kinds, width)).reshape(slots * kinds, width)
    grad_shrink = jnp.dot(activated.T, grad_rows, preferred_element_type=F32).astype(BF16)
    grad_expand = jnp.dot(expert_rows.T, grad_hidden, preferred_element_type=F32).astype(BF16)
    rows, grad_logits, phi_term = post(returned, tokens, cotangent, dispatch, combine)
    grad_phi = sum_everywhere(phi_term)
    layer_out, grad_tokens = tail(rows, dispatch, combine, grad_logits, slot_params)
    return (layer_out, grad_tokens, grad_phi, grad_expand[None], grad_shrink[None])


def solution(mesh):
    placed = (
        P(("gx", "gy"), None, None),
        P(),
        P(("gx", "gy"), None, None),
        P(("gx", "gy"), None, None),
        P(("gx", "gy"), None, None),
    )
    return jax.shard_map(
        body,
        mesh=mesh,
        in_specs=placed,
        out_specs=(
            P(("gx", "gy"), None, None),
            P(("gx", "gy"), None, None),
            P(),
            P(("gx", "gy"), None, None),
            P(("gx", "gy"), None, None),
        ),
        check_vma=False,
    )
```

```python
import jax
import jax.numpy as jnp
from jax import lax
from jax.experimental import pallas as pl
from jax.experimental.pallas import tpu as pltpu
from jax.sharding import PartitionSpec as P

AXES = ("gx", "gy")
BF16 = jnp.bfloat16
F32 = jnp.float32
TILE = 256
NN = (((1,), (0,)), ((), ()))
NT = (((1,), (1,)), ((), ()))
TN = (((0,), (0,)), ((), ()))


def mul(left, right, how=NN):
    return lax.dot_general(left, right, how, preferred_element_type=F32)


def in_space(array, space):
    return pltpu.with_memory_space_constraint(array, space)


def exchange(chunks):
    return lax.all_to_all(chunks, AXES, split_axis=0, concat_axis=0, tiled=True)


def one_hot_rows(kinds, grouped_to_mixed):
    span = TILE // kinds
    row = lax.broadcasted_iota(jnp.int32, (TILE, TILE), 0)
    column = lax.broadcasted_iota(jnp.int32, (TILE, TILE), 1)
    if grouped_to_mixed:
        source = (row % kinds) * span + row // kinds
    else:
        source = (row % span) * kinds + row // span
    return jnp.where(column == source, 1.0, 0.0).astype(BF16)


def pre_kernel(tokens_ref, cotangent_ref, params_ref, send_ref, dispatch_ref, combine_ref, rows_ref):
    step = pl.program_id(0)
    images = rows_ref.shape[0] // 2

    @pl.when(step < images)
    def _():
        one_image = tokens_ref[0]
        logits = mul(one_image, params_ref[...])
        down = jnp.exp(logits - jnp.max(logits, axis=0, keepdims=True))
        down = down / jnp.sum(down, axis=0, keepdims=True)
        across = jnp.exp(logits - jnp.max(logits, axis=1, keepdims=True))
        across = across / jnp.sum(across, axis=1, keepdims=True)
        dispatch_ref[0] = down
        combine_ref[0] = across
        rows_ref[step] = mul(down.T.astype(BF16), one_image).astype(BF16)
        rows_ref[images + step] = mul(across.T.astype(BF16), cotangent_ref[0]).astype(BF16)

    @pl.when(step >= images)
    def _():
        kinds = 2 * images
        span = TILE // kinds
        block = step - images
        grouped = rows_ref[:, pl.ds(block * span, span), :].reshape(TILE, rows_ref.shape[2])
        send_ref[...] = mul(one_hot_rows(kinds, True), grouped).astype(BF16)


def pre(tokens, cotangent, params):
    images, patches, width = tokens.shape
    slots = params.shape[1]
    kinds = 2 * images
    blocks = slots * kinds // TILE

    def image_map(step):
        return (jnp.minimum(step, images - 1), 0, 0)

    return pl.pallas_call(
        pre_kernel,
        grid=(images + blocks,),
        in_specs=[
            pl.BlockSpec((1, patches, width), image_map),
            pl.BlockSpec((1, patches, width), image_map),
            pl.BlockSpec((width, slots), lambda step: (0, 0)),
        ],
        out_specs=[
            pl.BlockSpec((TILE, width), lambda step: (jnp.maximum(step - images, 0), 0)),
            pl.BlockSpec((1, patches, slots), image_map),
            pl.BlockSpec((1, patches, slots), image_map),
        ],
        out_shape=[
            jax.ShapeDtypeStruct((slots * kinds, width), BF16),
            jax.ShapeDtypeStruct((images, patches, slots), F32),
            jax.ShapeDtypeStruct((images, patches, slots), F32),
        ],
        scratch_shapes=[pltpu.VMEM((kinds, slots, width), BF16)],
        compiler_params=pltpu.CompilerParams(vmem_limit_bytes=36 << 20),
        name="pre",
    )(*(in_space(array, pltpu.HBM) for array in (tokens, cotangent, params)))


def whole(*shapes):
    return [pl.BlockSpec(memory_space=pltpu.VMEM) for _ in shapes]


def expert_kernel(
    kinds,
    arrived_ref,
    expand_ref,
    shrink_ref,
    send_ref,
    kept_rows_ref,
    kept_grads_ref,
    activated_ref,
    hidden_grad_ref,
    rows_ref,
    grads_ref,
    rows_sem,
    grads_sem,
):
    half = TILE // 2
    blocks = arrived_ref.shape[0] // TILE
    width, hidden_width = expand_ref.shape
    step = 512

    order = one_hot_rows(kinds, False)
    for block in range(blocks):
        grouped = mul(order, arrived_ref[block * TILE : (block + 1) * TILE]).astype(BF16)
        rows_ref[block * half : (block + 1) * half] = grouped[:half]
        grads_ref[block * half : (block + 1) * half] = grouped[half:]
    keep_rows = pltpu.make_async_copy(rows_ref, kept_rows_ref, rows_sem)
    keep_grads = pltpu.make_async_copy(grads_ref, kept_grads_ref, grads_sem)
    keep_rows.start()
    keep_grads.start()

    def inner(index, carry):
        span = pl.ds(pl.multiple_of(index * step, step), step)
        hidden = mul(rows_ref[...], expand_ref[:, span])
        grad_activated = mul(grads_ref[...], shrink_ref[span, :], NT)
        cumulative = 0.5 * (1.0 + lax.erf(hidden * 0.7071067811865476))
        bell = jnp.exp(-0.5 * hidden * hidden) * 0.3989422804014327
        activated_ref[:, span] = (hidden * cumulative).astype(BF16)
        hidden_grad_ref[:, span] = (grad_activated * (cumulative + hidden * bell)).astype(BF16)
        return carry

    lax.fori_loop(0, hidden_width // step, inner, 0)
    back = one_hot_rows(kinds, True)

    def outer(index, carry):
        span = pl.ds(pl.multiple_of(index * step, step), step)
        result = mul(activated_ref[...], shrink_ref[:, span]).astype(BF16)
        input_grad = mul(hidden_grad_ref[...], expand_ref[span, :], NT).astype(BF16)
        for block in range(blocks):
            part = slice(block * half, (block + 1) * half)
            grouped = jnp.concatenate([result[part], input_grad[part]], axis=0)
            send_ref[block * TILE : (block + 1) * TILE, span] = mul(back, grouped).astype(BF16)
        return carry

    lax.fori_loop(0, width // step, outer, 0)
    keep_rows.wait()
    keep_grads.wait()


def expert(arrived, expand, shrink, kinds):
    total, width = arrived.shape
    hidden_width = expand.shape[1]
    rows = total // 2
    out_shape = [
        jax.ShapeDtypeStruct((total, width), BF16),
        pltpu.HBM((rows, width), BF16),
        pltpu.HBM((rows, width), BF16),
        jax.ShapeDtypeStruct((rows, hidden_width), BF16),
        jax.ShapeDtypeStruct((rows, hidden_width), BF16),
    ]
    vmem = pl.BlockSpec(memory_space=pltpu.VMEM)
    hbm = pl.BlockSpec(memory_space=pltpu.HBM)
    return pl.pallas_call(
        lambda *refs: expert_kernel(kinds, *refs),
        in_specs=whole(arrived, expand, shrink),
        out_specs=[vmem, hbm, hbm, vmem, vmem],
        out_shape=out_shape,
        scratch_shapes=[
            pltpu.VMEM((rows, width), BF16),
            pltpu.VMEM((rows, width), BF16),
            pltpu.SemaphoreType.DMA(()),
            pltpu.SemaphoreType.DMA(()),
        ],
        compiler_params=pltpu.CompilerParams(vmem_limit_bytes=32 << 20),
        name="expert",
    )(arrived, in_space(expand, pltpu.VMEM), in_space(shrink, pltpu.VMEM))


def weights_kernel(rows_ref, grads_ref, activated_ref, hidden_grad_ref, expand_ref, shrink_ref):
    expand_ref[...] = mul(rows_ref[...], hidden_grad_ref[...], TN).astype(BF16)
    shrink_ref[...] = mul(activated_ref[...], grads_ref[...], TN).astype(BF16)


def weights(rows, grads, activated, hidden_grad):
    count, width = rows.shape
    hidden_width = activated.shape[1]
    step = 512
    return pl.pallas_call(
        weights_kernel,
        grid=(hidden_width // step,),
        in_specs=[
            pl.BlockSpec((count, width), lambda index: (0, 0)),
            pl.BlockSpec((count, width), lambda index: (0, 0)),
            pl.BlockSpec((count, step), lambda index: (0, index)),
            pl.BlockSpec((count, step), lambda index: (0, index)),
        ],
        out_specs=[
            pl.BlockSpec((width, step), lambda index: (0, index)),
            pl.BlockSpec((step, width), lambda index: (index, 0)),
        ],
        out_shape=[
            jax.ShapeDtypeStruct((width, hidden_width), BF16),
            jax.ShapeDtypeStruct((hidden_width, width), BF16),
        ],
        compiler_params=pltpu.CompilerParams(vmem_limit_bytes=24 << 20),
        cost_estimate=pl.CostEstimate(
            flops=4 * count * width * hidden_width, bytes_accessed=14 << 20, transcendentals=0
        ),
        name="weights",
    )(*(in_space(array, pltpu.HBM) for array in (rows, grads, activated, hidden_grad)))


def post_kernel(
    images,
    arrived_ref,
    tokens_ref,
    cotangent_ref,
    dispatch_ref,
    combine_ref,
    kept_ref,
    grad_logits_ref,
    phi_ref,
    rows_ref,
    kept_sem,
):
    kinds, slots, width = rows_ref.shape
    span = TILE // kinds
    order = one_hot_rows(kinds, False)
    for block in range(slots // span):
        grouped = mul(order, arrived_ref[block * TILE : (block + 1) * TILE]).astype(BF16)
        rows_ref[:, block * span : (block + 1) * span, :] = grouped.reshape(kinds, span, width)
    keep = pltpu.make_async_copy(rows_ref, kept_ref, kept_sem)
    keep.start()
    total = jnp.zeros((slots, width), F32)
    for image in range(images):
        one_image = tokens_ref[image]
        down = dispatch_ref[image]
        across = combine_ref[image]
        grad_combine = mul(cotangent_ref[image], rows_ref[image], NT)
        grad_dispatch = mul(one_image, rows_ref[images + image], NT)
        grad_logits = down * (
            grad_dispatch - jnp.sum(down * grad_dispatch, axis=0, keepdims=True)
        ) + across * (grad_combine - jnp.sum(across * grad_combine, axis=1, keepdims=True))
        grad_logits_ref[image] = grad_logits.astype(BF16)
        total += mul(grad_logits.T.astype(BF16), one_image)
    phi_ref[...] = total.T.astype(BF16)
    keep.wait()


def post(arrived, tokens, cotangent, dispatch, combine):
    images, patches, width = tokens.shape
    slots = dispatch.shape[2]
    out_shape = [
        pltpu.HBM((2 * images, slots, width), BF16),
        jax.ShapeDtypeStruct((images, patches, slots), BF16),
        jax.ShapeDtypeStruct((width, slots), BF16),
    ]
    return pl.pallas_call(
        lambda *refs: post_kernel(images, *refs),
        in_specs=whole(arrived, tokens, cotangent, dispatch, combine),
        out_specs=[pl.BlockSpec(memory_space=pltpu.HBM)] + whole(*out_shape[1:]),
        out_shape=out_shape,
        scratch_shapes=[pltpu.VMEM(out_shape[0].shape, BF16), pltpu.SemaphoreType.DMA(())],
        compiler_params=pltpu.CompilerParams(vmem_limit_bytes=20 << 20),
        name="post",
    )(arrived, tokens, cotangent, dispatch, combine)


def tail_kernel(rows_ref, dispatch_ref, combine_ref, grad_logits_ref, params_ref, layer_ref, grad_ref):
    step = pl.program_id(0)
    images = pl.num_programs(0)
    layer_ref[0] = mul(combine_ref[step].astype(BF16), rows_ref[step]).astype(BF16)
    grad_ref[0] = (
        mul(dispatch_ref[step].astype(BF16), rows_ref[images + step])
        + mul(grad_logits_ref[step], params_ref[...], NT)
    ).astype(BF16)


def tail(rows, dispatch, combine, grad_logits, params):
    images, patches, slots = dispatch.shape
    width = rows.shape[2]
    image_map = lambda step: (step, 0, 0)
    out = jax.ShapeDtypeStruct((images, patches, width), BF16)
    return pl.pallas_call(
        tail_kernel,
        grid=(images,),
        in_specs=whole(rows, dispatch, combine, grad_logits, params),
        out_specs=[
            pl.BlockSpec((1, patches, width), image_map),
            pl.BlockSpec((1, patches, width), image_map),
        ],
        out_shape=[out, out],
        compiler_params=pltpu.CompilerParams(vmem_limit_bytes=16 << 20),
        cost_estimate=pl.CostEstimate(
            flops=6 * images * patches * slots * width, bytes_accessed=8 << 20, transcendentals=0
        ),
        name="tail",
    )(rows, dispatch, combine, grad_logits, params)


def sum_kernel(pieces_ref, copies_ref):
    own = jnp.sum(pieces_ref[...].astype(F32), axis=0, keepdims=True).astype(BF16)
    copies_ref[...] = jnp.broadcast_to(own, copies_ref.shape)


def widen_kernel(narrow_ref, wide_ref):
    wide_ref[...] = narrow_ref[...].astype(F32)


def sum_everywhere(partial):
    parts = lax.axis_size(AXES)
    rows, columns = partial.shape
    pieces = partial.reshape(parts, rows // parts, columns)
    copies = pl.pallas_call(
        sum_kernel,
        in_specs=whole(pieces),
        out_specs=whole(pieces)[0],
        out_shape=jax.ShapeDtypeStruct(pieces.shape, BF16),
        compiler_params=pltpu.CompilerParams(vmem_limit_bytes=4 << 20),
        name="sum",
    )(exchange(pieces))
    return pl.pallas_call(
        widen_kernel,
        in_specs=whole(partial),
        out_specs=whole(partial)[0],
        out_shape=jax.ShapeDtypeStruct(partial.shape, F32),
        compiler_params=pltpu.CompilerParams(vmem_limit_bytes=4 << 20),
        name="widen",
    )(exchange(copies).reshape(rows, columns))


def body(tokens, slot_params, expand_weight, shrink_weight, cotangent):
    images, _, width = tokens.shape
    slots = slot_params.shape[1]
    kinds = 2 * images
    send, dispatch, combine = pre(tokens, cotangent, slot_params)
    arrived = exchange(send.reshape(slots, kinds, width)).reshape(slots * kinds, width)
    send_back, expert_rows, grad_rows, activated, grad_hidden = expert(
        arrived, expand_weight[0], shrink_weight[0], kinds
    )
    returned = exchange(send_back.reshape(slots, kinds, width)).reshape(slots * kinds, width)
    grad_expand, grad_shrink = weights(expert_rows, grad_rows, activated, grad_hidden)
    rows, grad_logits, phi_term = post(returned, tokens, cotangent, dispatch, combine)
    grad_phi = sum_everywhere(phi_term)
    layer_out, grad_tokens = tail(rows, dispatch, combine, grad_logits, slot_params)
    return (layer_out, grad_tokens, grad_phi, grad_expand[None], grad_shrink[None])


def solution(mesh):
    placed = (
        P(("gx", "gy"), None, None),
        P(),
        P(("gx", "gy"), None, None),
        P(("gx", "gy"), None, None),
        P(("gx", "gy"), None, None),
    )
    return jax.shard_map(
        body,
        mesh=mesh,
        in_specs=placed,
        out_specs=(
            P(("gx", "gy"), None, None),
            P(("gx", "gy"), None, None),
            P(),
            P(("gx", "gy"), None, None),
            P(("gx", "gy"), None, None),
        ),
        check_vma=False,
    )
```

```python
import jax
import jax.numpy as jnp
from jax import lax
from jax.experimental import pallas as pl
from jax.experimental.pallas import tpu as pltpu
from jax.sharding import PartitionSpec as P

AXES = ("gx", "gy")
BF16 = jnp.bfloat16
F32 = jnp.float32
TILE = 256
NN = (((1,), (0,)), ((), ()))
NT = (((1,), (1,)), ((), ()))


def mul(left, right, how=NN):
    return lax.dot_general(left, right, how, preferred_element_type=F32)


def in_space(array, space):
    return pltpu.with_memory_space_constraint(array, space)


def exchange(chunks):
    return lax.all_to_all(chunks, AXES, split_axis=0, concat_axis=0, tiled=True)


def one_hot_rows(kinds, grouped_to_mixed):
    span = TILE // kinds
    row = lax.broadcasted_iota(jnp.int32, (TILE, TILE), 0)
    column = lax.broadcasted_iota(jnp.int32, (TILE, TILE), 1)
    if grouped_to_mixed:
        source = (row % kinds) * span + row // kinds
    else:
        source = (row % span) * kinds + row // span
    return jnp.where(column == source, 1.0, 0.0).astype(BF16)


def whole(*shapes):
    return [pl.BlockSpec(memory_space=pltpu.VMEM) for _ in shapes]


def pre_kernel(
    tokens_hbm,
    cotangent_hbm,
    params_hbm,
    send_ref,
    dispatch_ref,
    combine_ref,
    tokens_ref,
    cotangent_ref,
    params_ref,
    rows_ref,
    token_sems,
    cotangent_sems,
    params_sem,
):
    images, _, width = tokens_ref.shape
    slots = params_ref.shape[1]
    kinds = 2 * images
    get_params = pltpu.make_async_copy(params_hbm, params_ref, params_sem)
    get_tokens = [
        pltpu.make_async_copy(tokens_hbm.at[n], tokens_ref.at[n], token_sems.at[n])
        for n in range(images)
    ]
    get_cotangent = [
        pltpu.make_async_copy(cotangent_hbm.at[n], cotangent_ref.at[n], cotangent_sems.at[n])
        for n in range(images)
    ]
    get_params.start()
    for copy in get_tokens:
        copy.start()
    get_params.wait()
    for copy in get_tokens:
        copy.wait()
    for copy in get_cotangent:
        copy.start()
    patches = tokens_ref.shape[1]
    all_logits = mul(tokens_ref[...].reshape(images * patches, width), params_ref[...])
    for image in range(images):
        one_image = tokens_ref[image]
        logits = all_logits[image * patches : (image + 1) * patches]
        down = jnp.exp(logits - jnp.max(logits, axis=0, keepdims=True))
        down = down / jnp.sum(down, axis=0, keepdims=True)
        across = jnp.exp(logits - jnp.max(logits, axis=1, keepdims=True))
        across = across / jnp.sum(across, axis=1, keepdims=True)
        dispatch_ref[image] = down
        combine_ref[image] = across
        rows_ref[image] = mul(down.T.astype(BF16), one_image).astype(BF16)
    for copy in get_cotangent:
        copy.wait()
    for image in range(images):
        rows_ref[images + image] = mul(
            combine_ref[image].T.astype(BF16), cotangent_ref[image]
        ).astype(BF16)
    order = one_hot_rows(kinds, True)
    span = TILE // kinds
    for block in range(slots // span):
        grouped = rows_ref[:, block * span : (block + 1) * span, :].reshape(TILE, width)
        send_ref[block * TILE : (block + 1) * TILE] = mul(order, grouped).astype(BF16)


def pre(tokens, cotangent, params):
    images, patches, width = tokens.shape
    slots = params.shape[1]
    kinds = 2 * images
    out_shape = [
        jax.ShapeDtypeStruct((slots * kinds, width), BF16),
        jax.ShapeDtypeStruct((images, patches, slots), F32),
        jax.ShapeDtypeStruct((images, patches, slots), F32),
    ]
    arguments = (tokens, cotangent, params)
    return pl.pallas_call(
        pre_kernel,
        in_specs=[pl.BlockSpec(memory_space=pltpu.HBM) for _ in arguments],
        out_specs=whole(*out_shape),
        out_shape=out_shape,
        scratch_shapes=[
            pltpu.VMEM(tokens.shape, BF16),
            pltpu.VMEM(cotangent.shape, BF16),
            pltpu.VMEM(params.shape, BF16),
            pltpu.VMEM((kinds, slots, width), BF16),
            pltpu.SemaphoreType.DMA((images,)),
            pltpu.SemaphoreType.DMA((images,)),
            pltpu.SemaphoreType.DMA(()),
        ],
        compiler_params=pltpu.CompilerParams(vmem_limit_bytes=36 << 20),
        name="pre",
    )(*(in_space(array, pltpu.HBM) for array in arguments))


def expert_kernel(
    kinds,
    arrived_ref,
    expand_ref,
    shrink_ref,
    send_ref,
    kept_rows_ref,
    kept_grads_ref,
    activated_ref,
    hidden_grad_ref,
    rows_ref,
    grads_ref,
    rows_sem,
    grads_sem,
):
    half = TILE // 2
    blocks = arrived_ref.shape[0] // TILE
    width, hidden_width = expand_ref.shape
    step = 1024

    order = one_hot_rows(kinds, False)
    for block in range(blocks):
        grouped = mul(order, arrived_ref[block * TILE : (block + 1) * TILE]).astype(BF16)
        rows_ref[block * half : (block + 1) * half] = grouped[:half]
        grads_ref[block * half : (block + 1) * half] = grouped[half:]
    keep_rows = pltpu.make_async_copy(rows_ref, kept_rows_ref, rows_sem)
    keep_grads = pltpu.make_async_copy(grads_ref, kept_grads_ref, grads_sem)
    keep_rows.start()
    keep_grads.start()

    def inner(index, carry):
        span = pl.ds(pl.multiple_of(index * step, step), step)
        hidden = mul(rows_ref[...], expand_ref[:, span])
        grad_activated = mul(grads_ref[...], shrink_ref[span, :], NT)
        cumulative = 0.5 * (1.0 + lax.erf(hidden * 0.7071067811865476))
        bell = jnp.exp(-0.5 * hidden * hidden) * 0.3989422804014327
        activated_ref[:, span] = (hidden * cumulative).astype(BF16)
        hidden_grad_ref[:, span] = (grad_activated * (cumulative + hidden * bell)).astype(BF16)
        return carry

    lax.fori_loop(0, hidden_width // step, inner, 0, unroll=True)
    back = one_hot_rows(kinds, True)

    def outer(index, carry):
        span = pl.ds(pl.multiple_of(index * step, step), step)
        result = mul(activated_ref[...], shrink_ref[:, span]).astype(BF16)
        input_grad = mul(hidden_grad_ref[...], expand_ref[span, :], NT).astype(BF16)
        for block in range(blocks):
            part = slice(block * half, (block + 1) * half)
            grouped = jnp.concatenate([result[part], input_grad[part]], axis=0)
            send_ref[block * TILE : (block + 1) * TILE, span] = mul(back, grouped).astype(BF16)
        return carry

    lax.fori_loop(0, width // step, outer, 0, unroll=True)
    keep_rows.wait()
    keep_grads.wait()


def expert(arrived, expand, shrink, kinds):
    total, width = arrived.shape
    hidden_width = expand.shape[1]
    rows = total // 2
    out_shape = [
        jax.ShapeDtypeStruct((total, width), BF16),
        pltpu.HBM((rows, width), BF16),
        pltpu.HBM((rows, width), BF16),
        jax.ShapeDtypeStruct((rows, hidden_width), BF16),
        jax.ShapeDtypeStruct((rows, hidden_width), BF16),
    ]
    vmem = pl.BlockSpec(memory_space=pltpu.VMEM)
    hbm = pl.BlockSpec(memory_space=pltpu.HBM)
    return pl.pallas_call(
        lambda *refs: expert_kernel(kinds, *refs),
        in_specs=whole(arrived, expand, shrink),
        out_specs=[vmem, hbm, hbm, vmem, vmem],
        out_shape=out_shape,
        scratch_shapes=[
            pltpu.VMEM((rows, width), BF16),
            pltpu.VMEM((rows, width), BF16),
            pltpu.SemaphoreType.DMA(()),
            pltpu.SemaphoreType.DMA(()),
        ],
        compiler_params=pltpu.CompilerParams(vmem_limit_bytes=32 << 20),
        name="expert",
    )(arrived, in_space(expand, pltpu.VMEM), in_space(shrink, pltpu.VMEM))


def post_kernel(
    images,
    arrived_ref,
    tokens_ref,
    cotangent_ref,
    dispatch_ref,
    combine_ref,
    kept_ref,
    grad_logits_ref,
    phi_ref,
    rows_ref,
    kept_sem,
):
    kinds, slots, width = rows_ref.shape
    span = TILE // kinds
    order = one_hot_rows(kinds, False)
    for block in range(slots // span):
        grouped = mul(order, arrived_ref[block * TILE : (block + 1) * TILE]).astype(BF16)
        rows_ref[:, block * span : (block + 1) * span, :] = grouped.reshape(kinds, span, width)
    keep = pltpu.make_async_copy(rows_ref, kept_ref, kept_sem)
    keep.start()
    patches = tokens_ref.shape[1]
    parts = []
    for image in range(images):
        down = dispatch_ref[image]
        across = combine_ref[image]
        grad_combine = mul(cotangent_ref[image], rows_ref[image], NT)
        grad_dispatch = mul(tokens_ref[image], rows_ref[images + image], NT)
        grad_logits = down * (
            grad_dispatch - jnp.sum(down * grad_dispatch, axis=0, keepdims=True)
        ) + across * (grad_combine - jnp.sum(across * grad_combine, axis=1, keepdims=True))
        grad_logits_ref[image] = grad_logits.astype(BF16)
        parts.append(grad_logits.T.astype(BF16))
    all_tokens = tokens_ref[...].reshape(images * patches, width)
    total = mul(jnp.concatenate(parts, axis=1), all_tokens)
    phi_ref[...] = total.astype(BF16).T
    keep.wait()


def post(arrived, tokens, cotangent, dispatch, combine):
    images, patches, width = tokens.shape
    slots = dispatch.shape[2]
    out_shape = [
        pltpu.HBM((2 * images, slots, width), BF16),
        jax.ShapeDtypeStruct((images, patches, slots), BF16),
        jax.ShapeDtypeStruct((width, slots), BF16),
    ]
    return pl.pallas_call(
        lambda *refs: post_kernel(images, *refs),
        in_specs=whole(arrived, tokens, cotangent, dispatch, combine),
        out_specs=[pl.BlockSpec(memory_space=pltpu.HBM)] + whole(*out_shape[1:]),
        out_shape=out_shape,
        scratch_shapes=[pltpu.VMEM(out_shape[0].shape, BF16), pltpu.SemaphoreType.DMA(())],
        compiler_params=pltpu.CompilerParams(vmem_limit_bytes=20 << 20),
        name="post",
    )(arrived, tokens, cotangent, dispatch, combine)


CUT = 512


def flow(hbm_ref, vmem_ref, sems, pieces):
    return [
        (
            pltpu.make_async_copy(hbm_ref.at[piece], vmem_ref.at[piece], sems.at[index]),
            pltpu.make_async_copy(vmem_ref.at[piece], hbm_ref.at[piece], sems.at[index]),
        )
        for index, piece in enumerate(pieces)
    ]


def column_cuts(ref):
    return [(slice(None), pl.ds(start, CUT)) for start in range(0, ref.shape[1], CUT)]


def row_cuts(ref):
    return [(pl.ds(start, CUT), slice(None)) for start in range(0, ref.shape[0], CUT)]


def forward_finish_kernel(
    inputs_hbm,
    hidden_grad_hbm,
    slots_hbm,
    combine_ref,
    layer_hbm,
    expand_hbm,
    inputs_ref,
    hidden_grad_ref,
    slots_ref,
    layer_ref,
    expand_ref,
    inputs_sem,
    slots_sem,
    hidden_sems,
    expand_sems,
    layer_sems,
):
    images = combine_ref.shape[0]
    get_slots = pltpu.make_async_copy(slots_hbm.at[pl.ds(0, images)], slots_ref, slots_sem)
    get_inputs = pltpu.make_async_copy(inputs_hbm, inputs_ref, inputs_sem)
    hidden = flow(hidden_grad_hbm, hidden_grad_ref, hidden_sems, column_cuts(hidden_grad_ref))
    put_expand = flow(expand_hbm, expand_ref, expand_sems, column_cuts(expand_ref))
    put_layer = flow(layer_hbm, layer_ref, layer_sems, range(images))
    get_inputs.start()
    for get, _ in hidden:
        get.start()
    get_slots.start()
    get_inputs.wait()
    turned = inputs_ref[...].T
    for (get, _), (_, put), piece in zip(hidden, put_expand, column_cuts(expand_ref)):
        get.wait()
        expand_ref[piece] = mul(turned, hidden_grad_ref[piece]).astype(BF16)
        put.start()
    get_slots.wait()
    for image in range(images):
        layer_ref[image] = mul(combine_ref[image].astype(BF16), slots_ref[image]).astype(BF16)
        put_layer[image][1].start()
    for _, put in put_expand + put_layer:
        put.wait()


def backward_finish_kernel(
    grads_hbm,
    activated_hbm,
    slots_hbm,
    dispatch_ref,
    grad_logits_ref,
    params_ref,
    tokens_hbm,
    shrink_hbm,
    grads_ref,
    activated_ref,
    slots_ref,
    tokens_ref,
    shrink_ref,
    grads_sem,
    slots_sem,
    activated_sems,
    shrink_sems,
    tokens_sems,
):
    images = dispatch_ref.shape[0]
    get_slots = pltpu.make_async_copy(slots_hbm.at[pl.ds(images, images)], slots_ref, slots_sem)
    get_grads = pltpu.make_async_copy(grads_hbm, grads_ref, grads_sem)
    activated = flow(activated_hbm, activated_ref, activated_sems, column_cuts(activated_ref))
    put_shrink = flow(shrink_hbm, shrink_ref, shrink_sems, row_cuts(shrink_ref))
    put_tokens = flow(tokens_hbm, tokens_ref, tokens_sems, range(images))
    get_grads.start()
    for get, _ in activated:
        get.start()
    get_slots.start()
    back = params_ref[...].T
    get_grads.wait()
    pieces = zip(column_cuts(activated_ref), row_cuts(shrink_ref))
    for (get, _), (_, put), (source, target) in zip(activated, put_shrink, pieces):
        get.wait()
        shrink_ref[target] = mul(activated_ref[source].T, grads_ref[...]).astype(BF16)
        put.start()
    get_slots.wait()
    for image in range(images):
        factors = jnp.concatenate([dispatch_ref[image].astype(BF16), grad_logits_ref[image]], axis=1)
        sources = jnp.concatenate([slots_ref[image], back], axis=0)
        tokens_ref[image] = mul(factors, sources).astype(BF16)
        put_tokens[image][1].start()
    for _, put in put_shrink + put_tokens:
        put.wait()


def finish(kernel, name, held, near, outputs):
    images = near[0].shape[0]
    slots_shape = (images,) + held[2].shape[1:]
    return pl.pallas_call(
        kernel,
        in_specs=[pl.BlockSpec(memory_space=pltpu.HBM)] * len(held) + whole(*near),
        out_specs=[pl.BlockSpec(memory_space=pltpu.HBM)] * len(outputs),
        out_shape=[jax.ShapeDtypeStruct(shape, BF16) for shape in outputs],
        scratch_shapes=[
            pltpu.VMEM(held[0].shape, BF16),
            pltpu.VMEM(held[1].shape, BF16),
            pltpu.VMEM(slots_shape, BF16),
            *(pltpu.VMEM(shape, BF16) for shape in outputs),
            pltpu.SemaphoreType.DMA(()),
            pltpu.SemaphoreType.DMA(()),
            pltpu.SemaphoreType.DMA((held[1].shape[1] // CUT,)),
            pltpu.SemaphoreType.DMA((held[1].shape[1] // CUT,)),
            pltpu.SemaphoreType.DMA((images,)),
        ],
        compiler_params=pltpu.CompilerParams(vmem_limit_bytes=24 << 20),
        cost_estimate=pl.CostEstimate(flops=6 << 30, bytes_accessed=10 << 20, transcendentals=0),
        name=name,
    )(*(in_space(array, pltpu.HBM) for array in held), *near)


def sum_kernel(pieces_ref, copies_ref):
    own = jnp.sum(pieces_ref[...].astype(F32), axis=0, keepdims=True).astype(BF16)
    copies_ref[...] = jnp.broadcast_to(own, copies_ref.shape)


def widen_kernel(narrow_ref, wide_ref):
    wide_ref[...] = narrow_ref[...].astype(F32)


def add_pieces(pieces):
    return pl.pallas_call(
        sum_kernel,
        in_specs=whole(pieces),
        out_specs=whole(pieces)[0],
        out_shape=jax.ShapeDtypeStruct(pieces.shape, BF16),
        compiler_params=pltpu.CompilerParams(vmem_limit_bytes=4 << 20),
        name="sum",
    )(pieces)


def widen(narrow):
    return pl.pallas_call(
        widen_kernel,
        in_specs=whole(narrow),
        out_specs=whole(narrow)[0],
        out_shape=jax.ShapeDtypeStruct(narrow.shape, F32),
        compiler_params=pltpu.CompilerParams(vmem_limit_bytes=4 << 20),
        name="widen",
    )(narrow)


def body(tokens, slot_params, expand_weight, shrink_weight, cotangent):
    images, _, width = tokens.shape
    slots = slot_params.shape[1]
    kinds = 2 * images
    send, dispatch, combine = pre(tokens, cotangent, slot_params)
    arrived = exchange(send.reshape(slots, kinds, width)).reshape(slots * kinds, width)
    send_back, expert_rows, grad_rows, activated, grad_hidden = expert(
        arrived, expand_weight[0], shrink_weight[0], kinds
    )
    returned = exchange(send_back.reshape(slots, kinds, width)).reshape(slots * kinds, width)
    rows, grad_logits, phi_term = post(returned, tokens, cotangent, dispatch, combine)
    parts = lax.axis_size(AXES)
    pieces = exchange(phi_term.reshape(parts, width // parts, slots))
    layer_out, grad_expand = finish(
        forward_finish_kernel,
        "forward_finish",
        (expert_rows, grad_hidden, rows),
        (combine,),
        (tokens.shape, expand_weight.shape[1:]),
    )
    pieces, layer_out, grad_expand = lax.optimization_barrier((pieces, layer_out, grad_expand))
    copies = add_pieces(pieces)
    copies, activated = lax.optimization_barrier((copies, activated))
    grad_phi = widen(exchange(copies).reshape(width, slots))
    grad_tokens, grad_shrink = finish(
        backward_finish_kernel,
        "backward_finish",
        (grad_rows, activated, rows),
        (dispatch, grad_logits, slot_params),
        (tokens.shape, shrink_weight.shape[1:]),
    )
    return (layer_out, grad_tokens, grad_phi, grad_expand[None], grad_shrink[None])


def solution(mesh):
    placed = (
        P(("gx", "gy"), None, None),
        P(),
        P(("gx", "gy"), None, None),
        P(("gx", "gy"), None, None),
        P(("gx", "gy"), None, None),
    )
    return jax.shard_map(
        body,
        mesh=mesh,
        in_specs=placed,
        out_specs=(
            P(("gx", "gy"), None, None),
            P(("gx", "gy"), None, None),
            P(),
            P(("gx", "gy"), None, None),
            P(("gx", "gy"), None, None),
        ),
        check_vma=False,
    )
```

```python
import jax
import jax.numpy as jnp
from jax import lax
from jax.experimental import pallas as pl
from jax.experimental.pallas import tpu as pltpu
from jax.sharding import PartitionSpec as P

AXES = ("gx", "gy")
BF16 = jnp.bfloat16
F32 = jnp.float32
TILE = 256
NN = (((1,), (0,)), ((), ()))
NT = (((1,), (1,)), ((), ()))


def mul(left, right, how=NN):
    return lax.dot_general(left, right, how, preferred_element_type=F32)


def in_space(array, space):
    return pltpu.with_memory_space_constraint(array, space)


def exchange(chunks):
    return lax.all_to_all(chunks, AXES, split_axis=0, concat_axis=0, tiled=True)


def one_hot_rows(kinds, grouped_to_mixed):
    span = TILE // kinds
    row = lax.broadcasted_iota(jnp.int32, (TILE, TILE), 0)
    column = lax.broadcasted_iota(jnp.int32, (TILE, TILE), 1)
    if grouped_to_mixed:
        source = (row % kinds) * span + row // kinds
    else:
        source = (row % span) * kinds + row // span
    return jnp.where(column == source, 1.0, 0.0).astype(BF16)


def whole(*shapes):
    return [pl.BlockSpec(memory_space=pltpu.VMEM) for _ in shapes]


def pre_kernel(
    tokens_hbm,
    cotangent_hbm,
    params_hbm,
    send_ref,
    dispatch_ref,
    combine_ref,
    tokens_ref,
    cotangent_ref,
    params_ref,
    rows_ref,
    token_sems,
    cotangent_sems,
    params_sem,
):
    images, _, width = tokens_ref.shape
    slots = params_ref.shape[1]
    kinds = 2 * images
    get_params = pltpu.make_async_copy(params_hbm, params_ref, params_sem)
    get_tokens = [
        pltpu.make_async_copy(tokens_hbm.at[n], tokens_ref.at[n], token_sems.at[n])
        for n in range(images)
    ]
    get_cotangent = [
        pltpu.make_async_copy(cotangent_hbm.at[n], cotangent_ref.at[n], cotangent_sems.at[n])
        for n in range(images)
    ]
    get_params.start()
    for copy in get_tokens:
        copy.start()
    get_params.wait()
    for copy in get_tokens:
        copy.wait()
    for copy in get_cotangent:
        copy.start()
    patches = tokens_ref.shape[1]
    all_logits = mul(tokens_ref[...].reshape(images * patches, width), params_ref[...])
    for image in range(images):
        logits = all_logits[image * patches : (image + 1) * patches]
        down = jnp.exp(logits - jnp.max(logits, axis=0, keepdims=True))
        down = down * (1.0 / jnp.sum(down, axis=0, keepdims=True))
        dispatch_ref[image] = down
        rows_ref[image] = mul(down.astype(BF16).T, tokens_ref[image]).astype(BF16)
    all_across = jnp.exp(all_logits - jnp.max(all_logits, axis=1, keepdims=True))
    all_across = all_across * (1.0 / jnp.sum(all_across, axis=1, keepdims=True))
    for image in range(images):
        combine_ref[image] = all_across[image * patches : (image + 1) * patches]
    for copy in get_cotangent:
        copy.wait()
    for image in range(images):
        rows_ref[images + image] = mul(combine_ref[image].astype(BF16).T, cotangent_ref[image]).astype(BF16)
    order = one_hot_rows(kinds, True)
    span = TILE // kinds
    for block in range(slots // span):
        grouped = rows_ref[:, block * span : (block + 1) * span, :].reshape(TILE, width)
        send_ref[block * TILE : (block + 1) * TILE] = mul(order, grouped).astype(BF16)


def pre(tokens, cotangent, params):
    images, patches, width = tokens.shape
    slots = params.shape[1]
    kinds = 2 * images
    out_shape = [
        jax.ShapeDtypeStruct((slots * kinds, width), BF16),
        jax.ShapeDtypeStruct((images, patches, slots), F32),
        jax.ShapeDtypeStruct((images, patches, slots), F32),
    ]
    arguments = (tokens, cotangent, params)
    return pl.pallas_call(
        pre_kernel,
        in_specs=[pl.BlockSpec(memory_space=pltpu.HBM) for _ in arguments],
        out_specs=whole(*out_shape),
        out_shape=out_shape,
        scratch_shapes=[
            pltpu.VMEM(tokens.shape, BF16),
            pltpu.VMEM(cotangent.shape, BF16),
            pltpu.VMEM(params.shape, BF16),
            pltpu.VMEM((kinds, slots, width), BF16),
            pltpu.SemaphoreType.DMA((images,)),
            pltpu.SemaphoreType.DMA((images,)),
            pltpu.SemaphoreType.DMA(()),
        ],
        compiler_params=pltpu.CompilerParams(vmem_limit_bytes=36 << 20),
        name="pre",
    )(*(in_space(array, pltpu.HBM) for array in arguments))


def expert_kernel(
    kinds,
    arrived_ref,
    expand_ref,
    shrink_ref,
    send_ref,
    kept_rows_ref,
    kept_grads_ref,
    activated_ref,
    hidden_grad_ref,
    rows_ref,
    grads_ref,
    rows_sem,
    grads_sem,
):
    half = TILE // 2
    blocks = arrived_ref.shape[0] // TILE
    width, hidden_width = expand_ref.shape
    step = 1024

    group = kinds // 2
    low = lax.broadcasted_iota(jnp.int32, (1, kinds, 1), 1) < group
    for block in range(blocks):
        mixed = arrived_ref[block * TILE : (block + 1) * TILE].astype(F32)
        pairs = mixed.reshape(TILE // (2 * kinds), 2, kinds, width)
        left, right = pairs[:, 0], pairs[:, 1]
        part = slice(block * half, (block + 1) * half)
        first = jnp.where(low, left, pltpu.roll(right, group, 1))
        second = jnp.where(low, pltpu.roll(left, group, 1), right)
        rows_ref[part] = first.reshape(half, width).astype(BF16)
        grads_ref[part] = second.reshape(half, width).astype(BF16)
    keep_rows = pltpu.make_async_copy(rows_ref, kept_rows_ref, rows_sem)
    keep_grads = pltpu.make_async_copy(grads_ref, kept_grads_ref, grads_sem)
    keep_rows.start()
    keep_grads.start()

    def inner(index, carry):
        span = pl.ds(pl.multiple_of(index * step, step), step)
        hidden = mul(rows_ref[...], expand_ref[:, span])
        grad_activated = mul(grads_ref[...], shrink_ref[span, :], NT)
        cumulative = 0.5 * (1.0 + lax.erf(hidden * 0.7071067811865476))
        bell = jnp.exp(-0.5 * hidden * hidden) * 0.3989422804014327
        activated_ref[:, span] = (hidden * cumulative).astype(BF16)
        hidden_grad_ref[:, span] = (grad_activated * (cumulative + hidden * bell)).astype(BF16)
        return carry

    lax.fori_loop(0, hidden_width // step, inner, 0, unroll=True)
    def outer(index, carry):
        span = pl.ds(pl.multiple_of(index * step, step), step)
        result = mul(activated_ref[...], shrink_ref[:, span])
        input_grad = mul(hidden_grad_ref[...], expand_ref[span, :], NT)
        first = result.reshape(-1, kinds, step)
        second = input_grad.reshape(-1, kinds, step)
        left = jnp.where(low, first, pltpu.roll(second, group, 1))
        right = jnp.where(low, pltpu.roll(first, group, 1), second)
        mixed = jnp.stack([left, right], axis=1)
        send_ref[:, span] = mixed.reshape(-1, step).astype(BF16)
        return carry

    lax.fori_loop(0, width // step, outer, 0, unroll=True)
    keep_rows.wait()
    keep_grads.wait()


def expert(arrived, expand, shrink, kinds):
    total, width = arrived.shape
    hidden_width = expand.shape[1]
    rows = total // 2
    out_shape = [
        jax.ShapeDtypeStruct((total, width), BF16),
        pltpu.HBM((rows, width), BF16),
        pltpu.HBM((rows, width), BF16),
        jax.ShapeDtypeStruct((rows, hidden_width), BF16),
        jax.ShapeDtypeStruct((rows, hidden_width), BF16),
    ]
    vmem = pl.BlockSpec(memory_space=pltpu.VMEM)
    hbm = pl.BlockSpec(memory_space=pltpu.HBM)
    return pl.pallas_call(
        lambda *refs: expert_kernel(kinds, *refs),
        in_specs=whole(arrived, expand, shrink),
        out_specs=[vmem, hbm, hbm, vmem, vmem],
        out_shape=out_shape,
        scratch_shapes=[
            pltpu.VMEM((rows, width), BF16),
            pltpu.VMEM((rows, width), BF16),
            pltpu.SemaphoreType.DMA(()),
            pltpu.SemaphoreType.DMA(()),
        ],
        compiler_params=pltpu.CompilerParams(vmem_limit_bytes=32 << 20),
        name="expert",
    )(arrived, in_space(expand, pltpu.VMEM), in_space(shrink, pltpu.VMEM))


def post_kernel(
    images,
    arrived_ref,
    tokens_ref,
    cotangent_ref,
    dispatch_ref,
    combine_ref,
    kept_ref,
    grad_logits_ref,
    phi_ref,
    rows_ref,
    kept_sem,
):
    kinds, slots, width = rows_ref.shape
    span = TILE // kinds
    order = one_hot_rows(kinds, False)
    for block in range(slots // span):
        grouped = mul(order, arrived_ref[block * TILE : (block + 1) * TILE]).astype(BF16)
        rows_ref[:, block * span : (block + 1) * span, :] = grouped.reshape(kinds, span, width)
    keep = pltpu.make_async_copy(rows_ref, kept_ref, kept_sem)
    keep.start()
    patches = tokens_ref.shape[1]
    parts = []
    for image in range(images):
        down = dispatch_ref[image]
        across = combine_ref[image]
        grad_combine = mul(cotangent_ref[image], rows_ref[image], NT)
        grad_dispatch = mul(tokens_ref[image], rows_ref[images + image], NT)
        grad_logits = down * (
            grad_dispatch - jnp.sum(down * grad_dispatch, axis=0, keepdims=True)
        ) + across * (grad_combine - jnp.sum(across * grad_combine, axis=1, keepdims=True))
        grad_logits_ref[image] = grad_logits.astype(BF16)
        parts.append(grad_logits.astype(BF16).T)
    all_tokens = tokens_ref[...].reshape(images * patches, width)
    total = mul(jnp.concatenate(parts, axis=1), all_tokens)
    phi_ref[...] = total.astype(BF16).T
    keep.wait()


def post(arrived, tokens, cotangent, dispatch, combine):
    images, patches, width = tokens.shape
    slots = dispatch.shape[2]
    out_shape = [
        pltpu.HBM((2 * images, slots, width), BF16),
        jax.ShapeDtypeStruct((images, patches, slots), BF16),
        jax.ShapeDtypeStruct((width, slots), BF16),
    ]
    return pl.pallas_call(
        lambda *refs: post_kernel(images, *refs),
        in_specs=whole(arrived, tokens, cotangent, dispatch, combine),
        out_specs=[pl.BlockSpec(memory_space=pltpu.HBM)] + whole(*out_shape[1:]),
        out_shape=out_shape,
        scratch_shapes=[pltpu.VMEM(out_shape[0].shape, BF16), pltpu.SemaphoreType.DMA(())],
        compiler_params=pltpu.CompilerParams(vmem_limit_bytes=20 << 20),
        name="post",
    )(arrived, tokens, cotangent, dispatch, combine)


CUT = 512


def flow(hbm_ref, vmem_ref, sems, pieces):
    return [
        (
            pltpu.make_async_copy(hbm_ref.at[piece], vmem_ref.at[piece], sems.at[index]),
            pltpu.make_async_copy(vmem_ref.at[piece], hbm_ref.at[piece], sems.at[index]),
        )
        for index, piece in enumerate(pieces)
    ]


def column_cuts(ref):
    return [(slice(None), pl.ds(start, CUT)) for start in range(0, ref.shape[1], CUT)]


def row_cuts(ref):
    return [(pl.ds(start, CUT), slice(None)) for start in range(0, ref.shape[0], CUT)]


def forward_finish_kernel(
    inputs_hbm,
    hidden_grad_hbm,
    slots_hbm,
    combine_ref,
    layer_hbm,
    expand_hbm,
    inputs_ref,
    hidden_grad_ref,
    slots_ref,
    layer_ref,
    expand_ref,
    inputs_sem,
    slots_sem,
    hidden_sems,
    expand_sems,
    layer_sems,
):
    images = combine_ref.shape[0]
    get_slots = pltpu.make_async_copy(slots_hbm.at[pl.ds(0, images)], slots_ref, slots_sem)
    get_inputs = pltpu.make_async_copy(inputs_hbm, inputs_ref, inputs_sem)
    hidden = flow(hidden_grad_hbm, hidden_grad_ref, hidden_sems, column_cuts(hidden_grad_ref))
    put_expand = flow(expand_hbm, expand_ref, expand_sems, column_cuts(expand_ref))
    put_layer = flow(layer_hbm, layer_ref, layer_sems, range(images))
    get_inputs.start()
    for get, _ in hidden:
        get.start()
    get_slots.start()
    get_inputs.wait()
    turned = inputs_ref[...].T
    for (get, _), (_, put), piece in zip(hidden, put_expand, column_cuts(expand_ref)):
        get.wait()
        expand_ref[piece] = mul(turned, hidden_grad_ref[piece]).astype(BF16)
        put.start()
    get_slots.wait()
    for image in range(images):
        layer_ref[image] = mul(combine_ref[image].astype(BF16), slots_ref[image]).astype(BF16)
        put_layer[image][1].start()
    for _, put in put_expand + put_layer:
        put.wait()


def backward_finish_kernel(
    grads_hbm,
    activated_hbm,
    slots_hbm,
    dispatch_ref,
    grad_logits_ref,
    params_ref,
    tokens_hbm,
    shrink_hbm,
    grads_ref,
    activated_ref,
    slots_ref,
    tokens_ref,
    shrink_ref,
    grads_sem,
    slots_sem,
    activated_sems,
    shrink_sems,
    tokens_sems,
):
    images = dispatch_ref.shape[0]
    get_slots = pltpu.make_async_copy(slots_hbm.at[pl.ds(images, images)], slots_ref, slots_sem)
    get_grads = pltpu.make_async_copy(grads_hbm, grads_ref, grads_sem)
    activated = flow(activated_hbm, activated_ref, activated_sems, column_cuts(activated_ref))
    put_shrink = flow(shrink_hbm, shrink_ref, shrink_sems, row_cuts(shrink_ref))
    put_tokens = flow(tokens_hbm, tokens_ref, tokens_sems, range(images))
    get_grads.start()
    for get, _ in activated:
        get.start()
    get_slots.start()
    back = params_ref[...].T
    get_grads.wait()
    pieces = zip(column_cuts(activated_ref), row_cuts(shrink_ref))
    for (get, _), (_, put), (source, target) in zip(activated, put_shrink, pieces):
        get.wait()
        shrink_ref[target] = mul(activated_ref[source].T, grads_ref[...]).astype(BF16)
        put.start()
    get_slots.wait()
    for image in range(images):
        factors = jnp.concatenate([dispatch_ref[image].astype(BF16), grad_logits_ref[image]], axis=1)
        sources = jnp.concatenate([slots_ref[image], back], axis=0)
        tokens_ref[image] = mul(factors, sources).astype(BF16)
        put_tokens[image][1].start()
    for _, put in put_shrink + put_tokens:
        put.wait()


def finish(kernel, name, held, near, outputs):
    images = near[0].shape[0]
    slots_shape = (images,) + held[2].shape[1:]
    return pl.pallas_call(
        kernel,
        in_specs=[pl.BlockSpec(memory_space=pltpu.HBM)] * len(held) + whole(*near),
        out_specs=[pl.BlockSpec(memory_space=pltpu.HBM)] * len(outputs),
        out_shape=[jax.ShapeDtypeStruct(shape, BF16) for shape in outputs],
        scratch_shapes=[
            pltpu.VMEM(held[0].shape, BF16),
            pltpu.VMEM(held[1].shape, BF16),
            pltpu.VMEM(slots_shape, BF16),
            *(pltpu.VMEM(shape, BF16) for shape in outputs),
            pltpu.SemaphoreType.DMA(()),
            pltpu.SemaphoreType.DMA(()),
            pltpu.SemaphoreType.DMA((held[1].shape[1] // CUT,)),
            pltpu.SemaphoreType.DMA((held[1].shape[1] // CUT,)),
            pltpu.SemaphoreType.DMA((images,)),
        ],
        compiler_params=pltpu.CompilerParams(vmem_limit_bytes=24 << 20),
        cost_estimate=pl.CostEstimate(flops=6 << 30, bytes_accessed=10 << 20, transcendentals=0),
        name=name,
    )(*(in_space(array, pltpu.HBM) for array in held), *near)


def sum_kernel(pieces_ref, copies_ref):
    own = jnp.sum(pieces_ref[...].astype(F32), axis=0, keepdims=True).astype(BF16)
    copies_ref[...] = jnp.broadcast_to(own, copies_ref.shape)


def widen_kernel(narrow_ref, wide_ref):
    wide_ref[...] = narrow_ref[...].astype(F32)


def add_pieces(pieces):
    return pl.pallas_call(
        sum_kernel,
        in_specs=whole(pieces),
        out_specs=whole(pieces)[0],
        out_shape=jax.ShapeDtypeStruct(pieces.shape, BF16),
        compiler_params=pltpu.CompilerParams(vmem_limit_bytes=4 << 20),
        name="sum",
    )(pieces)


def widen(narrow):
    return pl.pallas_call(
        widen_kernel,
        in_specs=whole(narrow),
        out_specs=whole(narrow)[0],
        out_shape=jax.ShapeDtypeStruct(narrow.shape, F32),
        compiler_params=pltpu.CompilerParams(vmem_limit_bytes=4 << 20),
        name="widen",
    )(narrow)


def body(tokens, slot_params, expand_weight, shrink_weight, cotangent):
    images, _, width = tokens.shape
    slots = slot_params.shape[1]
    kinds = 2 * images
    send, dispatch, combine = pre(tokens, cotangent, slot_params)
    arrived = exchange(send.reshape(slots, kinds, width)).reshape(slots * kinds, width)
    send_back, expert_rows, grad_rows, activated, grad_hidden = expert(
        arrived, expand_weight[0], shrink_weight[0], kinds
    )
    returned = exchange(send_back.reshape(slots, kinds, width)).reshape(slots * kinds, width)
    rows, grad_logits, phi_term = post(returned, tokens, cotangent, dispatch, combine)
    parts = lax.axis_size(AXES)
    pieces = exchange(phi_term.reshape(parts, width // parts, slots))
    layer_out, grad_expand = finish(
        forward_finish_kernel,
        "forward_finish",
        (expert_rows, grad_hidden, rows),
        (combine,),
        (tokens.shape, expand_weight.shape[1:]),
    )
    pieces, layer_out, grad_expand = lax.optimization_barrier((pieces, layer_out, grad_expand))
    copies = add_pieces(pieces)
    copies, activated = lax.optimization_barrier((copies, activated))
    grad_phi = widen(exchange(copies).reshape(width, slots))
    grad_tokens, grad_shrink = finish(
        backward_finish_kernel,
        "backward_finish",
        (grad_rows, activated, rows),
        (dispatch, grad_logits, slot_params),
        (tokens.shape, shrink_weight.shape[1:]),
    )
    return (layer_out, grad_tokens, grad_phi, grad_expand[None], grad_shrink[None])


def solution(mesh):
    placed = (
        P(("gx", "gy"), None, None),
        P(),
        P(("gx", "gy"), None, None),
        P(("gx", "gy"), None, None),
        P(("gx", "gy"), None, None),
    )
    return jax.shard_map(
        body,
        mesh=mesh,
        in_specs=placed,
        out_specs=(
            P(("gx", "gy"), None, None),
            P(("gx", "gy"), None, None),
            P(),
            P(("gx", "gy"), None, None),
            P(("gx", "gy"), None, None),
        ),
        check_vma=False,
    )
```

```python
import jax
import jax.numpy as jnp
from jax import lax
from jax.experimental import pallas as pl
from jax.experimental.pallas import tpu as pltpu
from jax.sharding import Mesh, PartitionSpec as P

HELD = ("gx", "zh", "core")
AXES = ("core", "gx", "zh")
CORES = 2
BF16 = jnp.bfloat16
F32 = jnp.float32
TILE = 256
NN = (((1,), (0,)), ((), ()))
NT = (((1,), (1,)), ((), ()))


def mul(left, right, how=NN):
    return lax.dot_general(left, right, how, preferred_element_type=F32)


def in_space(array, space):
    return pltpu.with_memory_space_constraint(array, space)


def exchange(chunks):
    return lax.all_to_all(chunks, AXES, split_axis=0, concat_axis=0, tiled=True)


def one_hot_rows(kinds, grouped_to_mixed):
    span = TILE // kinds
    row = lax.broadcasted_iota(jnp.int32, (TILE, TILE), 0)
    column = lax.broadcasted_iota(jnp.int32, (TILE, TILE), 1)
    if grouped_to_mixed:
        source = (row % kinds) * span + row // kinds
    else:
        source = (row % span) * kinds + row // span
    return jnp.where(column == source, 1.0, 0.0).astype(BF16)


def whole(*shapes):
    return [pl.BlockSpec(memory_space=pltpu.VMEM) for _ in shapes]


def place_order(slots):
    slot = lax.broadcasted_iota(jnp.int32, (slots, slots), 0)
    place = lax.broadcasted_iota(jnp.int32, (slots, slots), 1)
    per_core = slots // CORES
    return jnp.where(slot == (place % per_core) * CORES + place // per_core, 1.0, 0.0).astype(BF16)


def pre_kernel(
    tokens_hbm,
    cotangent_hbm,
    params_hbm,
    send_ref,
    dispatch_ref,
    combine_ref,
    tokens_ref,
    cotangent_ref,
    params_ref,
    rows_ref,
    token_sems,
    cotangent_sems,
    params_sem,
):
    images, _, width = tokens_ref.shape
    slots = params_ref.shape[1]
    kinds = 2 * images
    get_params = pltpu.make_async_copy(params_hbm, params_ref, params_sem)
    get_tokens = [
        pltpu.make_async_copy(tokens_hbm.at[n], tokens_ref.at[n], token_sems.at[n])
        for n in range(images)
    ]
    get_cotangent = [
        pltpu.make_async_copy(cotangent_hbm.at[n], cotangent_ref.at[n], cotangent_sems.at[n])
        for n in range(images)
    ]
    get_params.start()
    for copy in get_tokens:
        copy.start()
    get_params.wait()
    params = mul(params_ref[...], place_order(slots)).astype(BF16)
    for copy in get_tokens:
        copy.wait()
    for copy in get_cotangent:
        copy.start()
    patches = tokens_ref.shape[1]
    all_logits = mul(tokens_ref[...].reshape(images * patches, width), params)
    for image in range(images):
        logits = all_logits[image * patches : (image + 1) * patches]
        down = jnp.exp(logits - jnp.max(logits, axis=0, keepdims=True))
        down = down * (1.0 / jnp.sum(down, axis=0, keepdims=True))
        dispatch_ref[image] = down
        rows_ref[image] = mul(down.astype(BF16).T, tokens_ref[image]).astype(BF16)
    all_across = jnp.exp(all_logits - jnp.max(all_logits, axis=1, keepdims=True))
    all_across = all_across * (1.0 / jnp.sum(all_across, axis=1, keepdims=True))
    for image in range(images):
        combine_ref[image] = all_across[image * patches : (image + 1) * patches]
    for copy in get_cotangent:
        copy.wait()
    for image in range(images):
        rows_ref[images + image] = mul(combine_ref[image].astype(BF16).T, cotangent_ref[image]).astype(BF16)
    order = one_hot_rows(kinds, True)
    span = TILE // kinds
    for block in range(slots // span):
        grouped = rows_ref[:, block * span : (block + 1) * span, :].reshape(TILE, width)
        send_ref[block * TILE : (block + 1) * TILE] = mul(order, grouped).astype(BF16)


def pre(tokens, cotangent, params):
    images, patches, width = tokens.shape
    slots = params.shape[1]
    kinds = 2 * images
    out_shape = [
        jax.ShapeDtypeStruct((slots * kinds, width), BF16),
        jax.ShapeDtypeStruct((images, patches, slots), F32),
        jax.ShapeDtypeStruct((images, patches, slots), F32),
    ]
    arguments = (tokens, cotangent, params)
    return pl.pallas_call(
        pre_kernel,
        in_specs=[pl.BlockSpec(memory_space=pltpu.HBM) for _ in arguments],
        out_specs=whole(*out_shape),
        out_shape=out_shape,
        scratch_shapes=[
            pltpu.VMEM(tokens.shape, BF16),
            pltpu.VMEM(cotangent.shape, BF16),
            pltpu.VMEM(params.shape, BF16),
            pltpu.VMEM((kinds, slots, width), BF16),
            pltpu.SemaphoreType.DMA((images,)),
            pltpu.SemaphoreType.DMA((images,)),
            pltpu.SemaphoreType.DMA(()),
        ],
        compiler_params=pltpu.CompilerParams(vmem_limit_bytes=36 << 20),
        name="pre",
    )(*(in_space(array, pltpu.HBM) for array in arguments))


def expert_kernel(
    kinds,
    arrived_ref,
    expand_ref,
    shrink_ref,
    send_ref,
    kept_rows_ref,
    kept_grads_ref,
    activated_ref,
    hidden_grad_ref,
    rows_ref,
    grads_ref,
    rows_sem,
    grads_sem,
):
    half = TILE // 2
    blocks = arrived_ref.shape[0] // TILE
    width, hidden_width = expand_ref.shape
    step = 1024

    group = kinds // 2
    low = lax.broadcasted_iota(jnp.int32, (1, kinds, 1), 1) < group
    for block in range(blocks):
        mixed = arrived_ref[block * TILE : (block + 1) * TILE].astype(F32)
        pairs = mixed.reshape(TILE // (2 * kinds), 2, kinds, width)
        left, right = pairs[:, 0], pairs[:, 1]
        part = slice(block * half, (block + 1) * half)
        first = jnp.where(low, left, pltpu.roll(right, group, 1))
        second = jnp.where(low, pltpu.roll(left, group, 1), right)
        rows_ref[part] = first.reshape(half, width).astype(BF16)
        grads_ref[part] = second.reshape(half, width).astype(BF16)
    keep_rows = pltpu.make_async_copy(rows_ref, kept_rows_ref, rows_sem)
    keep_grads = pltpu.make_async_copy(grads_ref, kept_grads_ref, grads_sem)
    keep_rows.start()
    keep_grads.start()

    def inner(index, carry):
        span = pl.ds(pl.multiple_of(index * step, step), step)
        hidden = mul(rows_ref[...], expand_ref[:, span])
        grad_activated = mul(grads_ref[...], shrink_ref[span, :], NT)
        cumulative = 0.5 * (1.0 + lax.erf(hidden * 0.7071067811865476))
        bell = jnp.exp(-0.5 * hidden * hidden) * 0.3989422804014327
        activated_ref[:, span] = (hidden * cumulative).astype(BF16)
        hidden_grad_ref[:, span] = (grad_activated * (cumulative + hidden * bell)).astype(BF16)
        return carry

    lax.fori_loop(0, hidden_width // step, inner, 0, unroll=True)
    def outer(index, carry):
        span = pl.ds(pl.multiple_of(index * step, step), step)
        result = mul(activated_ref[...], shrink_ref[:, span])
        input_grad = mul(hidden_grad_ref[...], expand_ref[span, :], NT)
        first = result.reshape(-1, kinds, step)
        second = input_grad.reshape(-1, kinds, step)
        left = jnp.where(low, first, pltpu.roll(second, group, 1))
        right = jnp.where(low, pltpu.roll(first, group, 1), second)
        mixed = jnp.stack([left, right], axis=1)
        send_ref[:, span] = mixed.reshape(-1, step).astype(BF16)
        return carry

    lax.fori_loop(0, width // step, outer, 0, unroll=True)
    keep_rows.wait()
    keep_grads.wait()


def expert(arrived, expand, shrink, kinds):
    total, width = arrived.shape
    hidden_width = expand.shape[1]
    rows = total // 2
    out_shape = [
        jax.ShapeDtypeStruct((total, width), BF16),
        pltpu.HBM((rows, width), BF16),
        pltpu.HBM((rows, width), BF16),
        jax.ShapeDtypeStruct((rows, hidden_width), BF16),
        jax.ShapeDtypeStruct((rows, hidden_width), BF16),
    ]
    vmem = pl.BlockSpec(memory_space=pltpu.VMEM)
    hbm = pl.BlockSpec(memory_space=pltpu.HBM)
    return pl.pallas_call(
        lambda *refs: expert_kernel(kinds, *refs),
        in_specs=whole(arrived, expand, shrink),
        out_specs=[vmem, hbm, hbm, vmem, vmem],
        out_shape=out_shape,
        scratch_shapes=[
            pltpu.VMEM((rows, width), BF16),
            pltpu.VMEM((rows, width), BF16),
            pltpu.SemaphoreType.DMA(()),
            pltpu.SemaphoreType.DMA(()),
        ],
        compiler_params=pltpu.CompilerParams(vmem_limit_bytes=32 << 20),
        name="expert",
    )(arrived, in_space(expand, pltpu.VMEM), in_space(shrink, pltpu.VMEM))


def post_kernel(
    images,
    arrived_ref,
    tokens_ref,
    cotangent_ref,
    dispatch_ref,
    combine_ref,
    kept_ref,
    grad_logits_ref,
    phi_hbm,
    rows_ref,
    phi_ref,
    kept_sem,
    phi_sems,
):
    kinds, slots, width = rows_ref.shape
    span = TILE // kinds
    order = one_hot_rows(kinds, False)
    for block in range(slots // span):
        grouped = mul(order, arrived_ref[block * TILE : (block + 1) * TILE]).astype(BF16)
        rows_ref[:, block * span : (block + 1) * span, :] = grouped.reshape(kinds, span, width)
    keep = pltpu.make_async_copy(rows_ref, kept_ref, kept_sem)
    keep.start()
    patches = tokens_ref.shape[1]
    parts = []
    for image in range(images):
        down = dispatch_ref[image]
        across = combine_ref[image]
        grad_combine = mul(cotangent_ref[image], rows_ref[image], NT)
        grad_dispatch = mul(tokens_ref[image], rows_ref[images + image], NT)
        grad_logits = down * (
            grad_dispatch - jnp.sum(down * grad_dispatch, axis=0, keepdims=True)
        ) + across * (grad_combine - jnp.sum(across * grad_combine, axis=1, keepdims=True))
        grad_logits_ref[image] = grad_logits.astype(BF16)
        parts.append(grad_logits.astype(BF16).T)
    all_tokens = tokens_ref[...].reshape(images * patches, width)
    turned = mul(place_order(slots), jnp.concatenate(parts, axis=1)).astype(BF16)
    cut = width // 2
    puts = []
    for index in range(2):
        span = slice(index * cut, (index + 1) * cut)
        phi_ref[span] = mul(turned, all_tokens[:, span]).astype(BF16).T
        put = pltpu.make_async_copy(phi_ref.at[pl.ds(index * cut, cut)], phi_hbm.at[pl.ds(index * cut, cut)], phi_sems.at[index])
        put.start()
        puts.append(put)
    for put in puts:
        put.wait()
    keep.wait()


def post(arrived, tokens, cotangent, dispatch, combine):
    images, patches, width = tokens.shape
    slots = dispatch.shape[2]
    out_shape = [
        pltpu.HBM((2 * images, slots, width), BF16),
        jax.ShapeDtypeStruct((images, patches, slots), BF16),
        pltpu.HBM((width, slots), BF16),
    ]
    return pl.pallas_call(
        lambda *refs: post_kernel(images, *refs),
        in_specs=whole(arrived, tokens, cotangent, dispatch, combine),
        out_specs=[
            pl.BlockSpec(memory_space=pltpu.HBM),
            pl.BlockSpec(memory_space=pltpu.VMEM),
            pl.BlockSpec(memory_space=pltpu.HBM),
        ],
        out_shape=out_shape,
        scratch_shapes=[
            pltpu.VMEM(out_shape[0].shape, BF16),
            pltpu.VMEM((width, slots), BF16),
            pltpu.SemaphoreType.DMA(()),
            pltpu.SemaphoreType.DMA((2,)),
        ],
        compiler_params=pltpu.CompilerParams(vmem_limit_bytes=20 << 20),
        name="post",
    )(arrived, tokens, cotangent, dispatch, combine)


CUT = 512


def flow(hbm_ref, vmem_ref, sems, pieces):
    return [
        (
            pltpu.make_async_copy(hbm_ref.at[piece], vmem_ref.at[piece], sems.at[index]),
            pltpu.make_async_copy(vmem_ref.at[piece], hbm_ref.at[piece], sems.at[index]),
        )
        for index, piece in enumerate(pieces)
    ]


def column_cuts(ref):
    return [(slice(None), pl.ds(start, CUT)) for start in range(0, ref.shape[1], CUT)]


def row_cuts(ref):
    return [(pl.ds(start, CUT), slice(None)) for start in range(0, ref.shape[0], CUT)]


def forward_finish_kernel(
    inputs_hbm,
    hidden_grad_hbm,
    slots_hbm,
    combine_ref,
    layer_hbm,
    expand_hbm,
    inputs_ref,
    hidden_grad_ref,
    slots_ref,
    layer_ref,
    expand_ref,
    inputs_sem,
    slots_sem,
    hidden_sems,
    expand_sems,
    layer_sems,
):
    images = combine_ref.shape[0]
    get_slots = pltpu.make_async_copy(slots_hbm.at[pl.ds(0, images)], slots_ref, slots_sem)
    get_inputs = pltpu.make_async_copy(inputs_hbm, inputs_ref, inputs_sem)
    hidden = flow(hidden_grad_hbm, hidden_grad_ref, hidden_sems, column_cuts(hidden_grad_ref))
    put_expand = flow(expand_hbm, expand_ref, expand_sems, column_cuts(expand_ref))
    put_layer = flow(layer_hbm, layer_ref, layer_sems, range(images))
    get_inputs.start()
    for get, _ in hidden:
        get.start()
    get_slots.start()
    get_inputs.wait()
    turned = inputs_ref[...].T
    for (get, _), (_, put), piece in zip(hidden, put_expand, column_cuts(expand_ref)):
        get.wait()
        expand_ref[piece] = mul(turned, hidden_grad_ref[piece]).astype(BF16)
        put.start()
    get_slots.wait()
    for image in range(images):
        layer_ref[image] = mul(combine_ref[image].astype(BF16), slots_ref[image]).astype(BF16)
        put_layer[image][1].start()
    for _, put in put_expand + put_layer:
        put.wait()


def backward_finish_kernel(
    grads_hbm,
    activated_hbm,
    slots_hbm,
    dispatch_ref,
    grad_logits_ref,
    params_ref,
    tokens_hbm,
    shrink_hbm,
    grads_ref,
    activated_ref,
    slots_ref,
    tokens_ref,
    shrink_ref,
    grads_sem,
    slots_sem,
    activated_sems,
    shrink_sems,
    tokens_sems,
):
    images = dispatch_ref.shape[0]
    get_slots = pltpu.make_async_copy(slots_hbm.at[pl.ds(images, images)], slots_ref, slots_sem)
    get_grads = pltpu.make_async_copy(grads_hbm, grads_ref, grads_sem)
    activated = flow(activated_hbm, activated_ref, activated_sems, column_cuts(activated_ref))
    put_shrink = flow(shrink_hbm, shrink_ref, shrink_sems, row_cuts(shrink_ref))
    put_tokens = flow(tokens_hbm, tokens_ref, tokens_sems, range(images))
    get_grads.start()
    for get, _ in activated:
        get.start()
    get_slots.start()
    back = mul(params_ref[...], place_order(params_ref.shape[1])).astype(BF16).T
    get_grads.wait()
    pieces = zip(column_cuts(activated_ref), row_cuts(shrink_ref))
    for (get, _), (_, put), (source, target) in zip(activated, put_shrink, pieces):
        get.wait()
        shrink_ref[target] = mul(activated_ref[source].T, grads_ref[...]).astype(BF16)
        put.start()
    get_slots.wait()
    for image in range(images):
        factors = jnp.concatenate([dispatch_ref[image].astype(BF16), grad_logits_ref[image]], axis=1)
        sources = jnp.concatenate([slots_ref[image], back], axis=0)
        tokens_ref[image] = mul(factors, sources).astype(BF16)
        put_tokens[image][1].start()
    for _, put in put_shrink + put_tokens:
        put.wait()


def finish(kernel, name, held, near, outputs):
    images = near[0].shape[0]
    slots_shape = (images,) + held[2].shape[1:]
    return pl.pallas_call(
        kernel,
        in_specs=[pl.BlockSpec(memory_space=pltpu.HBM)] * len(held) + whole(*near),
        out_specs=[pl.BlockSpec(memory_space=pltpu.HBM)] * len(outputs),
        out_shape=[jax.ShapeDtypeStruct(shape, BF16) for shape in outputs],
        scratch_shapes=[
            pltpu.VMEM(held[0].shape, BF16),
            pltpu.VMEM(held[1].shape, BF16),
            pltpu.VMEM(slots_shape, BF16),
            *(pltpu.VMEM(shape, BF16) for shape in outputs),
            pltpu.SemaphoreType.DMA(()),
            pltpu.SemaphoreType.DMA(()),
            pltpu.SemaphoreType.DMA((held[1].shape[1] // CUT,)),
            pltpu.SemaphoreType.DMA((held[1].shape[1] // CUT,)),
            pltpu.SemaphoreType.DMA((images,)),
        ],
        compiler_params=pltpu.CompilerParams(vmem_limit_bytes=24 << 20),
        cost_estimate=pl.CostEstimate(flops=6 << 30, bytes_accessed=10 << 20, transcendentals=0),
        name=name,
    )(*(in_space(array, pltpu.HBM) for array in held), *near)


def sum_kernel(pieces_ref, copies_ref):
    own = jnp.sum(pieces_ref[...].astype(F32), axis=0, keepdims=True).astype(BF16)
    copies_ref[...] = jnp.broadcast_to(own, copies_ref.shape)


def widen_kernel(narrow_ref, wide_ref):
    wide_ref[...] = narrow_ref[...].astype(F32)


def add_pieces(pieces):
    return pl.pallas_call(
        sum_kernel,
        in_specs=whole(pieces),
        out_specs=whole(pieces)[0],
        out_shape=jax.ShapeDtypeStruct(pieces.shape, BF16),
        compiler_params=pltpu.CompilerParams(vmem_limit_bytes=4 << 20),
        name="sum",
    )(pieces)


def widen(narrow):
    return pl.pallas_call(
        widen_kernel,
        in_specs=whole(narrow),
        out_specs=whole(narrow)[0],
        out_shape=jax.ShapeDtypeStruct(narrow.shape, F32),
        compiler_params=pltpu.CompilerParams(vmem_limit_bytes=4 << 20),
        name="widen",
    )(narrow)


def body(tokens, slot_params, expand_weight, shrink_weight, cotangent):
    images, _, width = tokens.shape
    slots = slot_params.shape[1]
    kinds = 2 * images
    send, dispatch, combine = pre(tokens, cotangent, slot_params)
    arrived = exchange(send.reshape(slots, kinds, width)).reshape(slots * kinds, width)
    send_back, expert_rows, grad_rows, activated, grad_hidden = expert(
        arrived, expand_weight[0], shrink_weight[0], kinds
    )
    returned = exchange(send_back.reshape(slots, kinds, width)).reshape(slots * kinds, width)
    rows, grad_logits, phi_term = post(returned, tokens, cotangent, dispatch, combine)
    parts = lax.axis_size(AXES)
    pieces = exchange(phi_term.reshape(parts, width // parts, slots))
    layer_out, grad_expand = finish(
        forward_finish_kernel,
        "forward_finish",
        (expert_rows, grad_hidden, rows),
        (combine,),
        (tokens.shape, expand_weight.shape[1:]),
    )
    pieces, layer_out, grad_expand = lax.optimization_barrier((pieces, layer_out, grad_expand))
    copies = add_pieces(pieces)
    copies, activated = lax.optimization_barrier((copies, activated))
    grad_phi = widen(exchange(copies).reshape(width, slots))
    grad_tokens, grad_shrink = finish(
        backward_finish_kernel,
        "backward_finish",
        (grad_rows, activated, rows),
        (dispatch, grad_logits, slot_params),
        (tokens.shape, shrink_weight.shape[1:]),
    )
    return (layer_out, grad_tokens, grad_phi, grad_expand[None], grad_shrink[None])


def solution(mesh):
    split = Mesh(mesh.devices.reshape(mesh.shape["gx"], -1, CORES), HELD)
    shared = P(HELD, None, None)
    return jax.shard_map(
        body,
        mesh=split,
        in_specs=(shared, P(), shared, shared, shared),
        out_specs=(shared, shared, P(), shared, shared),
        check_vma=False,
    )
```

```python
import jax
import jax.numpy as jnp
from jax import lax
from jax.experimental import pallas as pl
from jax.experimental.pallas import tpu as pltpu
from jax.sharding import Mesh, PartitionSpec as P

HELD = ("gx", "zh", "core")
AXES = ("core", "gx", "zh")
CORES = 2
BF16 = jnp.bfloat16
F32 = jnp.float32
TILE = 256
NN = (((1,), (0,)), ((), ()))
NT = (((1,), (1,)), ((), ()))


def mul(left, right, how=NN):
    return lax.dot_general(left, right, how, preferred_element_type=F32)


def in_space(array, space):
    return pltpu.with_memory_space_constraint(array, space)


def exchange(chunks):
    return lax.all_to_all(chunks, AXES, split_axis=0, concat_axis=0, tiled=True)


def one_hot_rows(kinds, grouped_to_mixed):
    span = TILE // kinds
    row = lax.broadcasted_iota(jnp.int32, (TILE, TILE), 0)
    column = lax.broadcasted_iota(jnp.int32, (TILE, TILE), 1)
    if grouped_to_mixed:
        source = (row % kinds) * span + row // kinds
    else:
        source = (row % span) * kinds + row // span
    return jnp.where(column == source, 1.0, 0.0).astype(BF16)


def whole(*shapes):
    return [pl.BlockSpec(memory_space=pltpu.VMEM) for _ in shapes]


def place_order(slots):
    slot = lax.broadcasted_iota(jnp.int32, (slots, slots), 0)
    place = lax.broadcasted_iota(jnp.int32, (slots, slots), 1)
    per_core = slots // CORES
    return jnp.where(slot == (place % per_core) * CORES + place // per_core, 1.0, 0.0).astype(BF16)


def pre_kernel(
    tokens_hbm,
    cotangent_hbm,
    params_hbm,
    send_ref,
    dispatch_ref,
    combine_ref,
    tokens_ref,
    cotangent_ref,
    params_ref,
    rows_ref,
    token_sems,
    cotangent_sems,
    params_sem,
):
    images, _, width = tokens_ref.shape
    slots = params_ref.shape[1]
    kinds = 2 * images
    get_params = pltpu.make_async_copy(params_hbm, params_ref, params_sem)
    get_tokens = [
        pltpu.make_async_copy(tokens_hbm.at[n], tokens_ref.at[n], token_sems.at[n])
        for n in range(images)
    ]
    get_cotangent = [
        pltpu.make_async_copy(cotangent_hbm.at[n], cotangent_ref.at[n], cotangent_sems.at[n])
        for n in range(images)
    ]
    get_params.start()
    for copy in get_tokens:
        copy.start()
    get_params.wait()
    params = mul(params_ref[...], place_order(slots)).astype(BF16)
    for copy in get_tokens:
        copy.wait()
    for copy in get_cotangent:
        copy.start()
    patches = tokens_ref.shape[1]
    all_logits = mul(tokens_ref[...].reshape(images * patches, width), params)
    for image in range(images):
        logits = all_logits[image * patches : (image + 1) * patches]
        down = jnp.exp(logits - jnp.max(logits, axis=0, keepdims=True))
        down = down * (1.0 / jnp.sum(down, axis=0, keepdims=True))
        dispatch_ref[image] = down
        rows_ref[image] = mul(down.astype(BF16).T, tokens_ref[image]).astype(BF16)
    all_across = jnp.exp(all_logits - jnp.max(all_logits, axis=1, keepdims=True))
    all_across = all_across * (1.0 / jnp.sum(all_across, axis=1, keepdims=True))
    for image in range(images):
        combine_ref[image] = all_across[image * patches : (image + 1) * patches]
    for copy in get_cotangent:
        copy.wait()
    for image in range(images):
        rows_ref[images + image] = mul(combine_ref[image].astype(BF16).T, cotangent_ref[image]).astype(BF16)
    order = one_hot_rows(kinds, True)
    span = TILE // kinds
    for block in range(slots // span):
        grouped = rows_ref[:, block * span : (block + 1) * span, :].reshape(TILE, width)
        send_ref[block * TILE : (block + 1) * TILE] = mul(order, grouped).astype(BF16)


def pre(tokens, cotangent, params):
    images, patches, width = tokens.shape
    slots = params.shape[1]
    kinds = 2 * images
    out_shape = [
        jax.ShapeDtypeStruct((slots * kinds, width), BF16),
        jax.ShapeDtypeStruct((images, patches, slots), F32),
        jax.ShapeDtypeStruct((images, patches, slots), F32),
    ]
    arguments = (tokens, cotangent, params)
    return pl.pallas_call(
        pre_kernel,
        in_specs=[pl.BlockSpec(memory_space=pltpu.HBM) for _ in arguments],
        out_specs=whole(*out_shape),
        out_shape=out_shape,
        scratch_shapes=[
            pltpu.VMEM(tokens.shape, BF16),
            pltpu.VMEM(cotangent.shape, BF16),
            pltpu.VMEM(params.shape, BF16),
            pltpu.VMEM((kinds, slots, width), BF16),
            pltpu.SemaphoreType.DMA((images,)),
            pltpu.SemaphoreType.DMA((images,)),
            pltpu.SemaphoreType.DMA(()),
        ],
        compiler_params=pltpu.CompilerParams(vmem_limit_bytes=36 << 20),
        name="pre",
    )(*(in_space(array, pltpu.HBM) for array in arguments))


def expert_kernel(
    kinds,
    arrived_ref,
    expand_ref,
    shrink_ref,
    send_ref,
    kept_rows_ref,
    kept_grads_ref,
    activated_ref,
    hidden_grad_ref,
    rows_ref,
    grads_ref,
    rows_sem,
    grads_sem,
):
    half = TILE // 2
    blocks = arrived_ref.shape[0] // TILE
    width, hidden_width = expand_ref.shape
    step = 1024

    group = kinds // 2
    low = lax.broadcasted_iota(jnp.int32, (1, kinds, 1), 1) < group
    for block in range(blocks):
        mixed = arrived_ref[block * TILE : (block + 1) * TILE].astype(F32)
        pairs = mixed.reshape(TILE // (2 * kinds), 2, kinds, width)
        left, right = pairs[:, 0], pairs[:, 1]
        part = slice(block * half, (block + 1) * half)
        first = jnp.where(low, left, pltpu.roll(right, group, 1))
        second = jnp.where(low, pltpu.roll(left, group, 1), right)
        rows_ref[part] = first.reshape(half, width).astype(BF16)
        grads_ref[part] = second.reshape(half, width).astype(BF16)
    keep_rows = pltpu.make_async_copy(rows_ref, kept_rows_ref, rows_sem)
    keep_grads = pltpu.make_async_copy(grads_ref, kept_grads_ref, grads_sem)
    keep_rows.start()
    keep_grads.start()

    def inner(index, carry):
        span = pl.ds(pl.multiple_of(index * step, step), step)
        hidden = mul(rows_ref[...], expand_ref[:, span])
        grad_activated = mul(grads_ref[...], shrink_ref[span, :], NT)
        cumulative = 0.5 * (1.0 + lax.erf(hidden * 0.7071067811865476))
        bell = jnp.exp(-0.5 * hidden * hidden) * 0.3989422804014327
        activated_ref[:, span] = (hidden * cumulative).astype(BF16)
        hidden_grad_ref[:, span] = (grad_activated * (cumulative + hidden * bell)).astype(BF16)
        return carry

    lax.fori_loop(0, hidden_width // step, inner, 0, unroll=True)
    def outer(index, carry):
        span = pl.ds(pl.multiple_of(index * step, step), step)
        result = mul(activated_ref[...], shrink_ref[:, span])
        input_grad = mul(hidden_grad_ref[...], expand_ref[span, :], NT)
        first = result.reshape(-1, kinds, step)
        second = input_grad.reshape(-1, kinds, step)
        left = jnp.where(low, first, pltpu.roll(second, group, 1))
        right = jnp.where(low, pltpu.roll(first, group, 1), second)
        mixed = jnp.stack([left, right], axis=1)
        send_ref[:, span] = mixed.reshape(-1, step).astype(BF16)
        return carry

    lax.fori_loop(0, width // step, outer, 0, unroll=True)
    keep_rows.wait()
    keep_grads.wait()


def expert(arrived, expand, shrink, kinds):
    total, width = arrived.shape
    hidden_width = expand.shape[1]
    rows = total // 2
    out_shape = [
        jax.ShapeDtypeStruct((total, width), BF16),
        pltpu.HBM((rows, width), BF16),
        pltpu.HBM((rows, width), BF16),
        jax.ShapeDtypeStruct((rows, hidden_width), BF16),
        jax.ShapeDtypeStruct((rows, hidden_width), BF16),
    ]
    vmem = pl.BlockSpec(memory_space=pltpu.VMEM)
    hbm = pl.BlockSpec(memory_space=pltpu.HBM)
    return pl.pallas_call(
        lambda *refs: expert_kernel(kinds, *refs),
        in_specs=whole(arrived, expand, shrink),
        out_specs=[vmem, hbm, hbm, vmem, vmem],
        out_shape=out_shape,
        scratch_shapes=[
            pltpu.VMEM((rows, width), BF16),
            pltpu.VMEM((rows, width), BF16),
            pltpu.SemaphoreType.DMA(()),
            pltpu.SemaphoreType.DMA(()),
        ],
        compiler_params=pltpu.CompilerParams(vmem_limit_bytes=32 << 20),
        name="expert",
    )(arrived, in_space(expand, pltpu.VMEM), in_space(shrink, pltpu.VMEM))


def post_kernel(
    images,
    arrived_ref,
    tokens_ref,
    cotangent_ref,
    dispatch_ref,
    combine_ref,
    kept_ref,
    grad_logits_ref,
    phi_hbm,
    rows_ref,
    phi_ref,
    kept_sem,
    phi_sems,
):
    kinds, slots, width = rows_ref.shape
    span = TILE // kinds
    order = one_hot_rows(kinds, False)
    for block in range(slots // span):
        grouped = mul(order, arrived_ref[block * TILE : (block + 1) * TILE]).astype(BF16)
        rows_ref[:, block * span : (block + 1) * span, :] = grouped.reshape(kinds, span, width)
    keep = pltpu.make_async_copy(rows_ref, kept_ref, kept_sem)
    keep.start()
    patches = tokens_ref.shape[1]
    parts = []
    for image in range(images):
        down = dispatch_ref[image]
        across = combine_ref[image]
        grad_combine = mul(cotangent_ref[image], rows_ref[image], NT)
        grad_dispatch = mul(tokens_ref[image], rows_ref[images + image], NT)
        grad_logits = down * (
            grad_dispatch - jnp.sum(down * grad_dispatch, axis=0, keepdims=True)
        ) + across * (grad_combine - jnp.sum(across * grad_combine, axis=1, keepdims=True))
        grad_logits_ref[image] = grad_logits.astype(BF16)
        parts.append(grad_logits.astype(BF16).T)
    all_tokens = tokens_ref[...].reshape(images * patches, width)
    turned = mul(place_order(slots), jnp.concatenate(parts, axis=1)).astype(BF16)
    cut = width // 2
    puts = []
    for index in range(2):
        span = slice(index * cut, (index + 1) * cut)
        phi_ref[span] = mul(turned, all_tokens[:, span]).astype(BF16).T
        put = pltpu.make_async_copy(phi_ref.at[pl.ds(index * cut, cut)], phi_hbm.at[pl.ds(index * cut, cut)], phi_sems.at[index])
        put.start()
        puts.append(put)
    for put in puts:
        put.wait()
    keep.wait()


def post(arrived, tokens, cotangent, dispatch, combine):
    images, patches, width = tokens.shape
    slots = dispatch.shape[2]
    out_shape = [
        pltpu.HBM((2 * images, slots, width), BF16),
        jax.ShapeDtypeStruct((images, patches, slots), BF16),
        pltpu.HBM((width, slots), BF16),
    ]
    return pl.pallas_call(
        lambda *refs: post_kernel(images, *refs),
        in_specs=whole(arrived, tokens, cotangent, dispatch, combine),
        out_specs=[
            pl.BlockSpec(memory_space=pltpu.HBM),
            pl.BlockSpec(memory_space=pltpu.VMEM),
            pl.BlockSpec(memory_space=pltpu.HBM),
        ],
        out_shape=out_shape,
        scratch_shapes=[
            pltpu.VMEM(out_shape[0].shape, BF16),
            pltpu.VMEM((width, slots), BF16),
            pltpu.SemaphoreType.DMA(()),
            pltpu.SemaphoreType.DMA((2,)),
        ],
        compiler_params=pltpu.CompilerParams(vmem_limit_bytes=20 << 20),
        name="post",
    )(arrived, tokens, cotangent, dispatch, combine)


CUT = 512


def flow(source_ref, target_ref, sems, pieces):
    return [
        pltpu.make_async_copy(source_ref.at[piece], target_ref.at[piece], sems.at[index])
        for index, piece in enumerate(pieces)
    ]


def column_cuts(ref):
    return [(slice(None), pl.ds(start, CUT)) for start in range(0, ref.shape[1], CUT)]


def row_cuts(ref):
    return [(pl.ds(start, CUT), slice(None)) for start in range(0, ref.shape[0], CUT)]


def forward_finish_kernel(
    inputs_hbm,
    hidden_grad_hbm,
    slots_hbm,
    combine_ref,
    layer_hbm,
    expand_hbm,
    inputs_ref,
    hidden_grad_ref,
    slots_ref,
    layer_ref,
    expand_ref,
    inputs_sem,
    slots_sem,
    hidden_sems,
    expand_sems,
    layer_sems,
):
    images = combine_ref.shape[0]
    get_slots = pltpu.make_async_copy(slots_hbm.at[pl.ds(0, images)], slots_ref, slots_sem)
    get_inputs = pltpu.make_async_copy(inputs_hbm, inputs_ref, inputs_sem)
    hidden = flow(hidden_grad_hbm, hidden_grad_ref, hidden_sems, column_cuts(hidden_grad_ref))
    put_expand = flow(expand_ref, expand_hbm, expand_sems, column_cuts(expand_ref))
    put_layer = flow(layer_ref, layer_hbm, layer_sems, range(images))
    get_inputs.start()
    for get in hidden:
        get.start()
    get_slots.start()
    get_inputs.wait()
    turned = inputs_ref[...].T
    for get, put, piece in zip(hidden, put_expand, column_cuts(expand_ref)):
        get.wait()
        expand_ref[piece] = mul(turned, hidden_grad_ref[piece]).astype(BF16)
        put.start()
    get_slots.wait()
    for image in range(images):
        layer_ref[image] = mul(combine_ref[image].astype(BF16), slots_ref[image]).astype(BF16)
        put_layer[image].start()
    for put in put_expand + put_layer:
        put.wait()


def backward_finish_kernel(
    grads_hbm,
    activated_hbm,
    slots_hbm,
    dispatch_ref,
    grad_logits_ref,
    params_ref,
    tokens_hbm,
    shrink_hbm,
    grads_ref,
    activated_ref,
    slots_ref,
    tokens_ref,
    shrink_ref,
    grads_sem,
    slots_sem,
    activated_sems,
    shrink_sems,
    tokens_sems,
):
    images = dispatch_ref.shape[0]
    get_slots = pltpu.make_async_copy(slots_hbm.at[pl.ds(images, images)], slots_ref, slots_sem)
    get_grads = pltpu.make_async_copy(grads_hbm, grads_ref, grads_sem)
    activated = flow(activated_hbm, activated_ref, activated_sems, column_cuts(activated_ref))
    put_shrink = flow(shrink_ref, shrink_hbm, shrink_sems, row_cuts(shrink_ref))
    put_tokens = flow(tokens_ref, tokens_hbm, tokens_sems, range(images))
    get_grads.start()
    for get in activated:
        get.start()
    get_slots.start()
    back = mul(params_ref[...], place_order(params_ref.shape[1])).astype(BF16).T
    get_grads.wait()
    pieces = zip(column_cuts(activated_ref), row_cuts(shrink_ref))
    for get, put, (source, target) in zip(activated, put_shrink, pieces):
        get.wait()
        shrink_ref[target] = mul(activated_ref[source].T, grads_ref[...]).astype(BF16)
        put.start()
    get_slots.wait()
    for image in range(images):
        factors = jnp.concatenate([dispatch_ref[image].astype(BF16), grad_logits_ref[image]], axis=1)
        sources = jnp.concatenate([slots_ref[image], back], axis=0)
        tokens_ref[image] = mul(factors, sources).astype(BF16)
        put_tokens[image].start()
    for put in put_shrink + put_tokens:
        put.wait()


def finish(kernel, name, held, near, outputs):
    images = near[0].shape[0]
    slots_shape = (images,) + held[2].shape[1:]
    return pl.pallas_call(
        kernel,
        in_specs=[pl.BlockSpec(memory_space=pltpu.HBM)] * len(held) + whole(*near),
        out_specs=[pl.BlockSpec(memory_space=pltpu.HBM)] * len(outputs),
        out_shape=[jax.ShapeDtypeStruct(shape, BF16) for shape in outputs],
        scratch_shapes=[
            pltpu.VMEM(held[0].shape, BF16),
            pltpu.VMEM(held[1].shape, BF16),
            pltpu.VMEM(slots_shape, BF16),
            *(pltpu.VMEM(shape, BF16) for shape in outputs),
            pltpu.SemaphoreType.DMA(()),
            pltpu.SemaphoreType.DMA(()),
            pltpu.SemaphoreType.DMA((held[1].shape[1] // CUT,)),
            pltpu.SemaphoreType.DMA((held[1].shape[1] // CUT,)),
            pltpu.SemaphoreType.DMA((images,)),
        ],
        compiler_params=pltpu.CompilerParams(vmem_limit_bytes=24 << 20),
        cost_estimate=pl.CostEstimate(flops=6 << 30, bytes_accessed=10 << 20, transcendentals=0),
        name=name,
    )(*(in_space(array, pltpu.HBM) for array in held), *near)


def sum_kernel(pieces_ref, copies_ref):
    own = jnp.sum(pieces_ref[...].astype(F32), axis=0, keepdims=True).astype(BF16)
    copies_ref[...] = jnp.broadcast_to(own, copies_ref.shape)


def widen_kernel(narrow_ref, wide_ref):
    wide_ref[...] = narrow_ref[...].astype(F32)


def add_pieces(pieces):
    return pl.pallas_call(
        sum_kernel,
        in_specs=whole(pieces),
        out_specs=whole(pieces)[0],
        out_shape=jax.ShapeDtypeStruct(pieces.shape, BF16),
        compiler_params=pltpu.CompilerParams(vmem_limit_bytes=4 << 20),
        name="sum",
    )(pieces)


def widen(narrow):
    return pl.pallas_call(
        widen_kernel,
        in_specs=whole(narrow),
        out_specs=whole(narrow)[0],
        out_shape=jax.ShapeDtypeStruct(narrow.shape, F32),
        compiler_params=pltpu.CompilerParams(vmem_limit_bytes=4 << 20),
        name="widen",
    )(narrow)


def body(tokens, slot_params, expand_weight, shrink_weight, cotangent):
    images, _, width = tokens.shape
    slots = slot_params.shape[1]
    kinds = 2 * images
    send, dispatch, combine = pre(tokens, cotangent, slot_params)
    arrived = exchange(send.reshape(slots, kinds, width)).reshape(slots * kinds, width)
    send_back, expert_rows, grad_rows, activated, grad_hidden = expert(
        arrived, expand_weight[0], shrink_weight[0], kinds
    )
    returned = exchange(send_back.reshape(slots, kinds, width)).reshape(slots * kinds, width)
    rows, grad_logits, phi_term = post(returned, tokens, cotangent, dispatch, combine)
    parts = lax.axis_size(AXES)
    pieces = exchange(phi_term.reshape(parts, width // parts, slots))
    layer_out, grad_expand = finish(
        forward_finish_kernel,
        "forward_finish",
        (expert_rows, grad_hidden, rows),
        (combine,),
        (tokens.shape, expand_weight.shape[1:]),
    )
    pieces, layer_out, grad_expand = lax.optimization_barrier((pieces, layer_out, grad_expand))
    copies = add_pieces(pieces)
    copies, activated = lax.optimization_barrier((copies, activated))
    grad_phi = widen(exchange(copies).reshape(width, slots))
    grad_tokens, grad_shrink = finish(
        backward_finish_kernel,
        "backward_finish",
        (grad_rows, activated, rows),
        (dispatch, grad_logits, slot_params),
        (tokens.shape, shrink_weight.shape[1:]),
    )
    return (layer_out, grad_tokens, grad_phi, grad_expand[None], grad_shrink[None])


def solution(mesh):
    split = Mesh(mesh.devices.reshape(mesh.shape["gx"], -1, CORES), HELD)
    shared = P(HELD, None, None)
    return jax.shard_map(
        body,
        mesh=split,
        in_specs=(shared, P(), shared, shared, shared),
        out_specs=(shared, shared, P(), shared, shared),
        check_vma=False,
    )
```

```python
import jax
import jax.numpy as jnp
from jax import lax
from jax.experimental import pallas as pl
from jax.experimental.pallas import tpu as pltpu
from jax.sharding import Mesh, PartitionSpec as P

HELD = ("gx", "zh", "core")
AXES = ("core", "gx", "zh")
CORES = 2
BF16 = jnp.bfloat16
F32 = jnp.float32
TILE = 256
NN = (((1,), (0,)), ((), ()))
NT = (((1,), (1,)), ((), ()))


def mul(left, right, how=NN):
    return lax.dot_general(left, right, how, preferred_element_type=F32)


def in_space(array, space):
    return pltpu.with_memory_space_constraint(array, space)


def exchange(chunks):
    return lax.all_to_all(chunks, AXES, split_axis=0, concat_axis=0, tiled=True)


def one_hot_rows(kinds, grouped_to_mixed):
    span = TILE // kinds
    row = lax.broadcasted_iota(jnp.int32, (TILE, TILE), 0)
    column = lax.broadcasted_iota(jnp.int32, (TILE, TILE), 1)
    if grouped_to_mixed:
        source = (row % kinds) * span + row // kinds
    else:
        source = (row % span) * kinds + row // span
    return jnp.where(column == source, 1.0, 0.0).astype(BF16)


def whole(*shapes):
    return [pl.BlockSpec(memory_space=pltpu.VMEM) for _ in shapes]


def place_order(slots):
    slot = lax.broadcasted_iota(jnp.int32, (slots, slots), 0)
    place = lax.broadcasted_iota(jnp.int32, (slots, slots), 1)
    per_core = slots // CORES
    return jnp.where(slot == (place % per_core) * CORES + place // per_core, 1.0, 0.0).astype(BF16)


def pre_kernel(
    tokens_hbm,
    cotangent_hbm,
    params_hbm,
    send_ref,
    dispatch_ref,
    combine_ref,
    tokens_ref,
    cotangent_ref,
    params_ref,
    rows_ref,
    token_sems,
    cotangent_sems,
    params_sem,
):
    images, _, width = tokens_ref.shape
    slots = params_ref.shape[1]
    kinds = 2 * images
    get_params = pltpu.make_async_copy(params_hbm, params_ref, params_sem)
    get_tokens = [
        pltpu.make_async_copy(tokens_hbm.at[n], tokens_ref.at[n], token_sems.at[n])
        for n in range(images)
    ]
    get_cotangent = [
        pltpu.make_async_copy(cotangent_hbm.at[n], cotangent_ref.at[n], cotangent_sems.at[n])
        for n in range(images)
    ]
    get_params.start()
    for copy in get_tokens:
        copy.start()
    get_params.wait()
    params = mul(params_ref[...], place_order(slots)).astype(BF16)
    for copy in get_tokens:
        copy.wait()
    for copy in get_cotangent:
        copy.start()
    patches = tokens_ref.shape[1]
    all_logits = mul(tokens_ref[...].reshape(images * patches, width), params)
    for image in range(images):
        logits = all_logits[image * patches : (image + 1) * patches]
        down = jnp.exp(logits - jnp.max(logits, axis=0, keepdims=True))
        down = down * (1.0 / jnp.sum(down, axis=0, keepdims=True))
        dispatch_ref[image] = down
        rows_ref[image] = mul(down.astype(BF16).T, tokens_ref[image]).astype(BF16)
    all_across = jnp.exp(all_logits - jnp.max(all_logits, axis=1, keepdims=True))
    all_across = all_across * (1.0 / jnp.sum(all_across, axis=1, keepdims=True))
    for image in range(images):
        combine_ref[image] = all_across[image * patches : (image + 1) * patches]
    for copy in get_cotangent:
        copy.wait()
    for image in range(images):
        rows_ref[images + image] = mul(combine_ref[image].astype(BF16).T, cotangent_ref[image]).astype(BF16)
    order = one_hot_rows(kinds, True)
    span = TILE // kinds
    for block in range(slots // span):
        grouped = rows_ref[:, block * span : (block + 1) * span, :].reshape(TILE, width)
        send_ref[block * TILE : (block + 1) * TILE] = mul(order, grouped).astype(BF16)


def pre(tokens, cotangent, params):
    images, patches, width = tokens.shape
    slots = params.shape[1]
    kinds = 2 * images
    out_shape = [
        jax.ShapeDtypeStruct((slots * kinds, width), BF16),
        jax.ShapeDtypeStruct((images, patches, slots), F32),
        jax.ShapeDtypeStruct((images, patches, slots), F32),
    ]
    arguments = (tokens, cotangent, params)
    return pl.pallas_call(
        pre_kernel,
        in_specs=[pl.BlockSpec(memory_space=pltpu.HBM) for _ in arguments],
        out_specs=whole(*out_shape),
        out_shape=out_shape,
        scratch_shapes=[
            pltpu.VMEM(tokens.shape, BF16),
            pltpu.VMEM(cotangent.shape, BF16),
            pltpu.VMEM(params.shape, BF16),
            pltpu.VMEM((kinds, slots, width), BF16),
            pltpu.SemaphoreType.DMA((images,)),
            pltpu.SemaphoreType.DMA((images,)),
            pltpu.SemaphoreType.DMA(()),
        ],
        compiler_params=pltpu.CompilerParams(vmem_limit_bytes=36 << 20),
        name="pre",
    )(*(in_space(array, pltpu.HBM) for array in arguments))


def expert_kernel(
    kinds,
    arrived_ref,
    expand_ref,
    shrink_ref,
    send_ref,
    kept_rows_ref,
    kept_grads_ref,
    activated_ref,
    hidden_grad_ref,
    rows_ref,
    grads_ref,
    rows_sem,
    grads_sem,
):
    half = TILE // 2
    blocks = arrived_ref.shape[0] // TILE
    width, hidden_width = expand_ref.shape
    step = 1024

    group = kinds // 2
    low = lax.broadcasted_iota(jnp.int32, (1, kinds, 1), 1) < group
    for block in range(blocks):
        mixed = arrived_ref[block * TILE : (block + 1) * TILE].astype(F32)
        pairs = mixed.reshape(TILE // (2 * kinds), 2, kinds, width)
        left, right = pairs[:, 0], pairs[:, 1]
        part = slice(block * half, (block + 1) * half)
        first = jnp.where(low, left, pltpu.roll(right, group, 1))
        second = jnp.where(low, pltpu.roll(left, group, 1), right)
        rows_ref[part] = first.reshape(half, width).astype(BF16)
        grads_ref[part] = second.reshape(half, width).astype(BF16)
    keep_rows = pltpu.make_async_copy(rows_ref, kept_rows_ref, rows_sem)
    keep_grads = pltpu.make_async_copy(grads_ref, kept_grads_ref, grads_sem)
    keep_rows.start()
    keep_grads.start()

    def inner(index, carry):
        span = pl.ds(pl.multiple_of(index * step, step), step)
        hidden = mul(rows_ref[...], expand_ref[:, span])
        grad_activated = mul(grads_ref[...], shrink_ref[span, :], NT)
        cumulative = 0.5 * (1.0 + lax.erf(hidden * 0.7071067811865476))
        bell = jnp.exp(-0.5 * hidden * hidden) * 0.3989422804014327
        activated_ref[:, span] = (hidden * cumulative).astype(BF16)
        hidden_grad_ref[:, span] = (grad_activated * (cumulative + hidden * bell)).astype(BF16)
        return carry

    lax.fori_loop(0, hidden_width // step, inner, 0, unroll=True)
    def outer(index, carry):
        span = pl.ds(pl.multiple_of(index * step, step), step)
        result = mul(activated_ref[...], shrink_ref[:, span])
        input_grad = mul(hidden_grad_ref[...], expand_ref[span, :], NT)
        first = result.reshape(-1, kinds, step)
        second = input_grad.reshape(-1, kinds, step)
        left = jnp.where(low, first, pltpu.roll(second, group, 1))
        right = jnp.where(low, pltpu.roll(first, group, 1), second)
        mixed = jnp.stack([left, right], axis=1)
        send_ref[:, span] = mixed.reshape(-1, step).astype(BF16)
        return carry

    lax.fori_loop(0, width // step, outer, 0, unroll=True)
    keep_rows.wait()
    keep_grads.wait()


def expert(arrived, expand, shrink, kinds):
    total, width = arrived.shape
    hidden_width = expand.shape[1]
    rows = total // 2
    out_shape = [
        jax.ShapeDtypeStruct((total, width), BF16),
        pltpu.HBM((rows, width), BF16),
        pltpu.HBM((rows, width), BF16),
        jax.ShapeDtypeStruct((rows, hidden_width), BF16),
        jax.ShapeDtypeStruct((rows, hidden_width), BF16),
    ]
    vmem = pl.BlockSpec(memory_space=pltpu.VMEM)
    hbm = pl.BlockSpec(memory_space=pltpu.HBM)
    return pl.pallas_call(
        lambda *refs: expert_kernel(kinds, *refs),
        in_specs=whole(arrived, expand, shrink),
        out_specs=[vmem, hbm, hbm, vmem, vmem],
        out_shape=out_shape,
        scratch_shapes=[
            pltpu.VMEM((rows, width), BF16),
            pltpu.VMEM((rows, width), BF16),
            pltpu.SemaphoreType.DMA(()),
            pltpu.SemaphoreType.DMA(()),
        ],
        compiler_params=pltpu.CompilerParams(vmem_limit_bytes=32 << 20),
        name="expert",
    )(arrived, in_space(expand, pltpu.VMEM), in_space(shrink, pltpu.VMEM))


def post_kernel(
    images,
    arrived_ref,
    tokens_ref,
    cotangent_ref,
    dispatch_ref,
    combine_ref,
    kept_ref,
    grad_logits_ref,
    phi_hbm,
    rows_ref,
    phi_ref,
    kept_sem,
    phi_sems,
):
    kinds, slots, width = rows_ref.shape
    span = TILE // kinds
    order = one_hot_rows(kinds, False)
    for block in range(slots // span):
        grouped = mul(order, arrived_ref[block * TILE : (block + 1) * TILE]).astype(BF16)
        rows_ref[:, block * span : (block + 1) * span, :] = grouped.reshape(kinds, span, width)
    keep = pltpu.make_async_copy(rows_ref, kept_ref, kept_sem)
    keep.start()
    patches = tokens_ref.shape[1]
    parts = []
    for image in range(images):
        down = dispatch_ref[image]
        across = combine_ref[image]
        grad_combine = mul(cotangent_ref[image], rows_ref[image], NT)
        grad_dispatch = mul(tokens_ref[image], rows_ref[images + image], NT)
        grad_logits = down * (
            grad_dispatch - jnp.sum(down * grad_dispatch, axis=0, keepdims=True)
        ) + across * (grad_combine - jnp.sum(across * grad_combine, axis=1, keepdims=True))
        grad_logits_ref[image] = grad_logits.astype(BF16)
        parts.append(grad_logits.astype(BF16).T)
    all_tokens = tokens_ref[...].reshape(images * patches, width)
    turned = jnp.concatenate(parts, axis=1)
    cut = width // 2
    puts = []
    for index in range(2):
        span = slice(index * cut, (index + 1) * cut)
        phi_ref[span] = mul(turned, all_tokens[:, span]).astype(BF16).T
        put = pltpu.make_async_copy(phi_ref.at[pl.ds(index * cut, cut)], phi_hbm.at[pl.ds(index * cut, cut)], phi_sems.at[index])
        put.start()
        puts.append(put)
    for put in puts:
        put.wait()
    keep.wait()


def post(arrived, tokens, cotangent, dispatch, combine):
    images, patches, width = tokens.shape
    slots = dispatch.shape[2]
    out_shape = [
        pltpu.HBM((2 * images, slots, width), BF16),
        jax.ShapeDtypeStruct((images, patches, slots), BF16),
        pltpu.HBM((width, slots), BF16),
    ]
    return pl.pallas_call(
        lambda *refs: post_kernel(images, *refs),
        in_specs=whole(arrived, tokens, cotangent, dispatch, combine),
        out_specs=[
            pl.BlockSpec(memory_space=pltpu.HBM),
            pl.BlockSpec(memory_space=pltpu.VMEM),
            pl.BlockSpec(memory_space=pltpu.HBM),
        ],
        out_shape=out_shape,
        scratch_shapes=[
            pltpu.VMEM(out_shape[0].shape, BF16),
            pltpu.VMEM((width, slots), BF16),
            pltpu.SemaphoreType.DMA(()),
            pltpu.SemaphoreType.DMA((2,)),
        ],
        compiler_params=pltpu.CompilerParams(vmem_limit_bytes=20 << 20),
        name="post",
    )(arrived, tokens, cotangent, dispatch, combine)


CUT = 512


def flow(source_ref, target_ref, sems, pieces):
    return [
        pltpu.make_async_copy(source_ref.at[piece], target_ref.at[piece], sems.at[index])
        for index, piece in enumerate(pieces)
    ]


def column_cuts(ref):
    return [(slice(None), pl.ds(start, CUT)) for start in range(0, ref.shape[1], CUT)]


def row_cuts(ref):
    return [(pl.ds(start, CUT), slice(None)) for start in range(0, ref.shape[0], CUT)]


def forward_finish_kernel(
    inputs_hbm,
    hidden_grad_hbm,
    slots_hbm,
    combine_ref,
    layer_hbm,
    expand_hbm,
    inputs_ref,
    hidden_grad_ref,
    slots_ref,
    layer_ref,
    expand_ref,
    inputs_sem,
    slots_sem,
    hidden_sems,
    expand_sems,
    layer_sems,
):
    images = combine_ref.shape[0]
    get_slots = pltpu.make_async_copy(slots_hbm.at[pl.ds(0, images)], slots_ref, slots_sem)
    get_inputs = pltpu.make_async_copy(inputs_hbm, inputs_ref, inputs_sem)
    hidden = flow(hidden_grad_hbm, hidden_grad_ref, hidden_sems, column_cuts(hidden_grad_ref))
    put_expand = flow(expand_ref, expand_hbm, expand_sems, column_cuts(expand_ref))
    put_layer = flow(layer_ref, layer_hbm, layer_sems, range(images))
    get_inputs.start()
    for get in hidden:
        get.start()
    get_slots.start()
    get_inputs.wait()
    turned = inputs_ref[...].T
    for get, put, piece in zip(hidden, put_expand, column_cuts(expand_ref)):
        get.wait()
        expand_ref[piece] = mul(turned, hidden_grad_ref[piece]).astype(BF16)
        put.start()
    get_slots.wait()
    for image in range(images):
        layer_ref[image] = mul(combine_ref[image].astype(BF16), slots_ref[image]).astype(BF16)
        put_layer[image].start()
    for put in put_expand + put_layer:
        put.wait()


def backward_finish_kernel(
    grads_hbm,
    activated_hbm,
    slots_hbm,
    dispatch_ref,
    grad_logits_ref,
    params_ref,
    tokens_hbm,
    shrink_hbm,
    grads_ref,
    activated_ref,
    slots_ref,
    tokens_ref,
    shrink_ref,
    grads_sem,
    slots_sem,
    activated_sems,
    shrink_sems,
    tokens_sems,
):
    images = dispatch_ref.shape[0]
    get_slots = pltpu.make_async_copy(slots_hbm.at[pl.ds(images, images)], slots_ref, slots_sem)
    get_grads = pltpu.make_async_copy(grads_hbm, grads_ref, grads_sem)
    activated = flow(activated_hbm, activated_ref, activated_sems, column_cuts(activated_ref))
    put_shrink = flow(shrink_ref, shrink_hbm, shrink_sems, row_cuts(shrink_ref))
    put_tokens = flow(tokens_ref, tokens_hbm, tokens_sems, range(images))
    get_grads.start()
    for get in activated:
        get.start()
    get_slots.start()
    back = mul(params_ref[...], place_order(params_ref.shape[1])).astype(BF16).T
    get_grads.wait()
    pieces = zip(column_cuts(activated_ref), row_cuts(shrink_ref))
    for get, put, (source, target) in zip(activated, put_shrink, pieces):
        get.wait()
        shrink_ref[target] = mul(activated_ref[source].T, grads_ref[...]).astype(BF16)
        put.start()
    get_slots.wait()
    for image in range(images):
        factors = jnp.concatenate([dispatch_ref[image].astype(BF16), grad_logits_ref[image]], axis=1)
        sources = jnp.concatenate([slots_ref[image], back], axis=0)
        tokens_ref[image] = mul(factors, sources).astype(BF16)
        put_tokens[image].start()
    for put in put_shrink + put_tokens:
        put.wait()


def finish(kernel, name, held, near, outputs):
    images = near[0].shape[0]
    slots_shape = (images,) + held[2].shape[1:]
    return pl.pallas_call(
        kernel,
        in_specs=[pl.BlockSpec(memory_space=pltpu.HBM)] * len(held) + whole(*near),
        out_specs=[pl.BlockSpec(memory_space=pltpu.HBM)] * len(outputs),
        out_shape=[jax.ShapeDtypeStruct(shape, BF16) for shape in outputs],
        scratch_shapes=[
            pltpu.VMEM(held[0].shape, BF16),
            pltpu.VMEM(held[1].shape, BF16),
            pltpu.VMEM(slots_shape, BF16),
            *(pltpu.VMEM(shape, BF16) for shape in outputs),
            pltpu.SemaphoreType.DMA(()),
            pltpu.SemaphoreType.DMA(()),
            pltpu.SemaphoreType.DMA((held[1].shape[1] // CUT,)),
            pltpu.SemaphoreType.DMA((held[1].shape[1] // CUT,)),
            pltpu.SemaphoreType.DMA((images,)),
        ],
        compiler_params=pltpu.CompilerParams(vmem_limit_bytes=24 << 20),
        cost_estimate=pl.CostEstimate(flops=6 << 30, bytes_accessed=10 << 20, transcendentals=0),
        name=name,
    )(*(in_space(array, pltpu.HBM) for array in held), *near)


def sum_kernel(pieces_ref, copies_ref):
    own = jnp.sum(pieces_ref[...].astype(F32), axis=0).astype(BF16)
    own = mul(own, place_order(own.shape[1]), NT).astype(BF16)
    copies_ref[...] = jnp.broadcast_to(own[None], copies_ref.shape)


def widen_kernel(narrow_ref, wide_ref):
    wide_ref[...] = narrow_ref[...].astype(F32)


def add_pieces(pieces):
    return pl.pallas_call(
        sum_kernel,
        in_specs=whole(pieces),
        out_specs=whole(pieces)[0],
        out_shape=jax.ShapeDtypeStruct(pieces.shape, BF16),
        compiler_params=pltpu.CompilerParams(vmem_limit_bytes=4 << 20),
        name="sum",
    )(pieces)


def widen(narrow):
    return pl.pallas_call(
        widen_kernel,
        in_specs=whole(narrow),
        out_specs=whole(narrow)[0],
        out_shape=jax.ShapeDtypeStruct(narrow.shape, F32),
        compiler_params=pltpu.CompilerParams(vmem_limit_bytes=4 << 20),
        name="widen",
    )(narrow)


def body(tokens, slot_params, expand_weight, shrink_weight, cotangent):
    images, _, width = tokens.shape
    slots = slot_params.shape[1]
    kinds = 2 * images
    send, dispatch, combine = pre(tokens, cotangent, slot_params)
    arrived = exchange(send.reshape(slots, kinds, width)).reshape(slots * kinds, width)
    send_back, expert_rows, grad_rows, activated, grad_hidden = expert(
        arrived, expand_weight[0], shrink_weight[0], kinds
    )
    returned = exchange(send_back.reshape(slots, kinds, width)).reshape(slots * kinds, width)
    rows, grad_logits, phi_term = post(returned, tokens, cotangent, dispatch, combine)
    parts = lax.axis_size(AXES)
    pieces = exchange(phi_term.reshape(parts, width // parts, slots))
    layer_out, grad_expand = finish(
        forward_finish_kernel,
        "forward_finish",
        (expert_rows, grad_hidden, rows),
        (combine,),
        (tokens.shape, expand_weight.shape[1:]),
    )
    pieces, layer_out, grad_expand = lax.optimization_barrier((pieces, layer_out, grad_expand))
    copies = add_pieces(pieces)
    copies, activated = lax.optimization_barrier((copies, activated))
    grad_phi = widen(exchange(copies).reshape(width, slots))
    grad_tokens, grad_shrink = finish(
        backward_finish_kernel,
        "backward_finish",
        (grad_rows, activated, rows),
        (dispatch, grad_logits, slot_params),
        (tokens.shape, shrink_weight.shape[1:]),
    )
    return (layer_out, grad_tokens, grad_phi, grad_expand[None], grad_shrink[None])


def solution(mesh):
    split = Mesh(mesh.devices.reshape(mesh.shape["gx"], -1, CORES), HELD)
    shared = P(HELD, None, None)
    return jax.shard_map(
        body,
        mesh=split,
        in_specs=(shared, P(), shared, shared, shared),
        out_specs=(shared, shared, P(), shared, shared),
        check_vma=False,
    )
```
